256 devices in a mesh: blk: 64 (over z_hi, y, x, core), grp: 4 (over z_lo).
Axes of the slice: x: 4, y: 4, z: 8 (z_hi: 2, z_lo: 4; z = z_hi * 4 + z_lo), core: 2. Of those that a mesh axis runs over, the one named last changes fastest.
Arguments:
- a_tiles: bfloat16 [2048, 64, 1024], P(('blk', 'grp')), may hold values from -0.75 to 0.75
- a_cols: int32 [2048, 16], P(('blk', 'grp')), may hold values from 0 to 2047, as said below
- p_tiles: bfloat16 [2048, 64, 256], P(('blk', 'grp')), may hold values from -0.75 to 0.75
- route_list: int32 [2048, 256], P(('blk', 'grp')), may hold values from 0 to 255, as said below
- out_slot: int32 [256, 256], P(('blk', 'grp')), may hold values from 0 to 127, as said below
Outputs:
- coarse_blocks: float32 [32768, 4096], P(('blk', 'grp'))
The draws below stay inside these ranges and needn't reach their ends.
Inputs may be any that keep to these rules, and one draw needn't show every extreme that they name: `a_cols`: fine block row f is held by device f // 8 of blk+grp. Every entry in the rows of one device names a fine block row held by a device with the same grp index, and among the 128 entries of one device's rows exactly 2 name rows held by each blk index. `route_list`: A value o * 64 + p sends the partial block to send position p for the device with grp index o and the same blk index. For each device and each o, no position at or above a count is used, the count being at least 16, and 64 for one o of each device. `out_slot`: entry o * 64 + p of row d is the output block, among the 128 of the device with grp index o and the blk index of device d, into which send position p of device d adds; each output block index stands exactly 4 * 64 // 128 times in a row.
All inputs are finite; a program needn't handle non-finite values.
Results may differ from the reference program's by a relative error of at most 0.0029.
Values may be sent and summed in bfloat16 or wider, within the bound.
A program may use at most 128 MiB of HBM per device.

```python
import jax
import jax.numpy as jnp
from jax import lax

TILE = 64
RF = 8
KA = 16
KP = 4
CAP = 64
OSLOT = 128
NF = 2048
N_BLK = 64
N_GRP = 4


def draw_a_cols(key, part):
    base = jax.random.fold_in(key, 101)
    tile_count = RF * KA
    per_peer = tile_count // N_BLK

    def per_device(device):
        device_key = jax.random.fold_in(base, device)
        key_perm, key_row = jax.random.split(device_key)
        ranks = jax.random.permutation(key_perm, tile_count)
        peer_index = ranks // per_peer
        row_index = jax.random.randint(key_row, (tile_count,), 0, RF)
        row_index = jnp.where(ranks == tile_count - 1, RF - 1, jnp.where(ranks == 0, 0, row_index))
        group_index = device % N_GRP
        return ((peer_index * N_GRP + group_index) * RF + row_index).astype(jnp.int32)
    spread = jax.vmap(per_device)(jnp.arange(N_BLK * N_GRP, dtype=jnp.int32))
    return spread.reshape(N_BLK * N_GRP * RF, KA)


def draw_route_list(key, part):
    base = jax.random.fold_in(key, 202)
    part_count = RF * KP * KA * KP
    shift_key = jax.random.fold_in(base, 7)
    shift = jax.random.randint(shift_key, (), 0, N_GRP)
    lowest = max(1, CAP // 4)

    def per_device(device):
        device_key = jax.random.fold_in(base, device + 1000)
        key_count, key_owner, key_pos, key_pick = jax.random.split(device_key, 4)
        counts = jax.random.randint(key_count, (N_GRP,), lowest, CAP + 1)
        fullest = (device + shift) % N_GRP
        counts = jnp.where(jnp.arange(N_GRP) == fullest, CAP, counts)
        owners = jax.random.randint(key_owner, (part_count,), 0, N_GRP)
        positions = jax.random.randint(key_pos, (part_count,), 0, counts[owners])
        chosen = jax.random.randint(key_pick, (), 0, part_count)
        other = (chosen + 1) % part_count
        places = jnp.arange(part_count)
        values = owners * CAP + positions
        values = jnp.where(places == chosen, fullest * CAP + CAP - 1, values)
        values = jnp.where(places == other, 0, values)
        return values.astype(jnp.int32)
    spread = jax.vmap(per_device)(jnp.arange(N_BLK * N_GRP, dtype=jnp.int32))
    return spread.reshape(N_BLK * N_GRP * RF, KP * KA * KP)


def draw_out_slot(key, part):
    base = jax.random.fold_in(key, 303)

    def per_device(device):
        device_key = jax.random.fold_in(base, device)
        ranks = jax.random.permutation(device_key, N_GRP * CAP)
        return (ranks % OSLOT).astype(jnp.int32)
    return jax.vmap(per_device)(jnp.arange(N_BLK * N_GRP, dtype=jnp.int32))


def steps_of(key, extent, pieces, smallest, high):
    def one(position, shards_of):
        heights = jax.random.uniform(jax.random.fold_in(jax.random.fold_in(key, 6), position), (shards_of,), jnp.float32, smallest / len(pieces), high / len(pieces))
        return jnp.repeat(jnp.exp(heights), extent[position] // shards_of).reshape((-1,) + (1,) * (len(extent) - position - 1))

    loudness = one(*pieces[0])
    for cut in pieces[1:]:
        loudness = loudness * one(*cut)
    return loudness


def gaussian(rng, extent, scale, most, pieces=(), held_as=jnp.bfloat16):
    gain = steps_of(rng, extent, pieces, -0.22, 0.18) if pieces else 1.0
    values = jax.random.normal(rng, extent, jnp.float32) * scale * gain
    return jnp.minimum(jnp.maximum(values, -most), most).astype(held_as)


def setup_inputs(seed: int = 0) -> dict:
    seeds = jax.random.split(jax.random.key(seed), 6)
    a_tiles = gaussian(seeds[0], (NF, TILE, KA * TILE), TILE ** -0.5, 0.75, ((0, 256),))
    a_cols = draw_a_cols(jax.random.fold_in(seeds[5], 71), 0)
    p_tiles = gaussian(seeds[2], (NF, TILE, KP * TILE), TILE ** -0.5, 0.75, ((0, 256),))
    route_list = draw_route_list(jax.random.fold_in(seeds[5], 71), 0)
    out_slot = draw_out_slot(jax.random.fold_in(seeds[5], 71), 0)
    return {"a_tiles": a_tiles, "a_cols": a_cols, "p_tiles": p_tiles, "route_list": route_list, "out_slot": out_slot}


def reference(a_tiles, a_cols, p_tiles, route_list, out_slot):
    devices = N_BLK * N_GRP
    a_blocks = a_tiles.reshape(devices * RF, TILE, KA, TILE)

    def device_step(current, device):
        first_row = (device * RF).astype(jnp.int32)
        row_tiles = lax.dynamic_slice_in_dim(a_blocks, first_row, RF, 0)
        col_lists = lax.dynamic_slice_in_dim(a_cols, first_row, RF, 0)
        panel = jnp.take(p_tiles, col_lists.reshape(-1), axis=0).reshape(RF, KA, TILE, KP * TILE)
        product = jnp.einsum("rtks,rkso->rkto", row_tiles.astype(jnp.float32), panel.astype(jnp.float32)).astype(jnp.bfloat16)
        own_rows = lax.dynamic_slice_in_dim(p_tiles, first_row, RF, 0).reshape(RF, TILE, KP, TILE)
        y_five = product.reshape(RF, KA, TILE, KP, TILE)
        partials = jnp.einsum("irsc,ikrqd->iskqcd", own_rows.astype(jnp.float32), y_five.astype(jnp.float32))
        partials = partials.reshape(RF * KP * KA * KP, TILE * TILE)
        destination = lax.dynamic_slice_in_dim(route_list, first_row, RF, 0).reshape(-1)
        slot_row = lax.dynamic_index_in_dim(out_slot, device, 0, keepdims=False)
        segment = ((device // N_GRP) * N_GRP + destination // CAP) * OSLOT + jnp.take(slot_row, destination)
        return current.at[segment.astype(jnp.int32)].add(partials), None

    initial = jnp.zeros((devices * OSLOT, TILE * TILE), jnp.float32)
    summed, _ = lax.scan(device_step, initial, jnp.arange(devices, dtype=jnp.int32))
    return summed
```

```python
import heapq

import jax
import jax.numpy as jnp
from jax import lax
from jax.experimental import pallas as pl
from jax.experimental.pallas import tpu as pltpu
from jax.sharding import PartitionSpec as P

TILE = 64
RF = 8
KA = 16
KP = 4
CAP = 64
OSLOT = 128
GRP = 4
SLOTS = RF * KA
POS = GRP * CAP
MESH = pl.DeviceIdType.MESH
NACC = 4


def low_lanes(shape):
    return lax.broadcasted_iota(jnp.int32, shape, 1) < TILE


def turned(block):
    return pltpu.roll(block.astype(jnp.float32), TILE, 1).astype(jnp.bfloat16)


def product_kernel(cols_ref, route_ref, me_ref, a_ref, p_ref, panel_ref, send_ref, own_ref, picked, weights, *rest):
    accs, sems = rest[:NACC], rest[NACC]

    @pl.loop(0, SLOTS)
    def _(m):
        i = m // KA
        pltpu.make_async_copy(panel_ref.at[cols_ref[m]], picked.at[m], sems.at[i]).start()

    @pl.loop(0, POS)
    def _(r):
        for acc in accs:
            acc[r] = jnp.zeros((32, 128), jnp.float32)

    low = low_lanes((TILE, 128))
    zero = jnp.zeros((TILE, 128), jnp.bfloat16)

    @pl.loop(0, RF)
    def _(i):
        pltpu.make_async_copy(panel_ref.at[pl.ds(0, KA)], picked.at[pl.ds(i * KA, KA)], sems.at[i]).wait()
        for half in range(2):
            pair = p_ref[i, :, half * 128:(half + 1) * 128]
            back = turned(pair)
            even, odd = 2 * half * 128, (2 * half + 1) * 128
            weights[0:TILE, even:even + 128] = jnp.where(low, pair, zero)
            weights[TILE:128, even:even + 128] = jnp.where(low, zero, back)
            weights[0:TILE, odd:odd + 128] = jnp.where(low, back, zero)
            weights[TILE:128, odd:odd + 128] = jnp.where(low, zero, pair)

        @pl.loop(0, KA // 2)
        def _(kk):
            pair = a_ref[i, :, pl.ds(pl.multiple_of(kk * 128, 128), 128)]
            back = turned(pair)
            for parity in range(2):
                first, second = (pair, back) if parity == 0 else (back, pair)
                tile = jnp.concatenate([jnp.where(low, first, zero), jnp.where(low, zero, second)], axis=0)
                k = kk * 2 + parity
                y = lax.dot_general(
                    picked[i * KA + k], tile, (((1,), (1,)), ((), ())), preferred_element_type=jnp.float32
                ).astype(jnp.bfloat16)
                for s in range(KP):
                    w = jnp.dot(y, weights[:, s * 128:(s + 1) * 128], preferred_element_type=jnp.float32)
                    for q in range(KP):
                        r = route_ref[i * 256 + (s * KA + k) * KP + q]
                        acc = accs[(s * KP + q) % NACC]
                        acc[r] = acc[r] + w[q * 32:(q + 1) * 32]

    @pl.loop(0, POS)
    def _(r):
        total = accs[0][r]
        for acc in accs[1:]:
            total = total + acc[r]
        send_ref[r] = total.astype(jnp.bfloat16)

    @pl.loop(0, CAP)
    def _(p):
        r = me_ref[0] * CAP + p
        total = accs[0][r]
        for acc in accs[1:]:
            total = total + acc[r]
        own_ref[p] = total


def product(cols, route, me, a_tiles, p_tiles, panel):
    smem = pl.BlockSpec(memory_space=pltpu.SMEM)
    vmem = pl.BlockSpec(memory_space=pltpu.VMEM)
    return pl.pallas_call(
        product_kernel,
        out_shape=(
            jax.ShapeDtypeStruct((POS, 32, 128), jnp.bfloat16),
            jax.ShapeDtypeStruct((CAP, 32, 128), jnp.float32),
        ),
        in_specs=[smem, smem, smem, vmem, vmem, pl.BlockSpec(memory_space=pl.ANY)],
        out_specs=(vmem, vmem),
        scratch_shapes=[
            pltpu.VMEM((SLOTS, 128, 128), jnp.bfloat16),
            pltpu.VMEM((128, 512), jnp.bfloat16),
        ]
        + [pltpu.VMEM((POS, 32, 128), jnp.float32)] * NACC
        + [pltpu.SemaphoreType.DMA((RF,))],
        compiler_params=pltpu.CompilerParams(vmem_limit_bytes=48 * 1024 * 1024),
        name="product",
    )(cols, route, me, a_tiles, p_tiles, panel)


def exchange_kernel(send_ref, slot_ref, recv_ref, rslot_ref, send_sems, recv_sems, slot_send, slot_recv):
    blk, me = lax.axis_index("blk"), lax.axis_index("grp")
    barrier = pltpu.get_barrier_semaphore()

    def partner(j):
        flip_low = me + 1 - 2 * lax.rem(me, 2)
        if j == 1:
            return flip_low
        flip_high = lax.rem(me + 2, 4)
        if j == 2:
            return flip_high
        return 3 - me

    for j in (1, 2, 3):
        pl.semaphore_signal(barrier, inc=1, device_id=(blk, partner(j)), device_id_type=MESH)
    pl.semaphore_wait(barrier, 3)
    copies = []
    for j in (3, 2, 1):
        other = partner(j)
        copies.append(pltpu.make_async_remote_copy(
            src_ref=slot_ref, dst_ref=rslot_ref.at[j - 1], send_sem=slot_send.at[j - 1], recv_sem=slot_recv.at[j - 1],
            device_id=(blk, other), device_id_type=MESH))
        copies.append(pltpu.make_async_remote_copy(
            src_ref=send_ref.at[pl.ds(other * CAP, CAP)], dst_ref=recv_ref.at[j - 1],
            send_sem=send_sems.at[j - 1], recv_sem=recv_sems.at[j - 1], device_id=(blk, other), device_id_type=MESH))
    for copy in copies:
        copy.start()
    for copy in copies:
        copy.wait()


def exchange(send, slots):
    anywhere = pl.BlockSpec(memory_space=pl.ANY)
    return pl.pallas_call(
        exchange_kernel,
        out_shape=(
            jax.ShapeDtypeStruct((3, CAP, 32, 128), jnp.bfloat16),
            jax.ShapeDtypeStruct((3, 2, 128), jnp.int32),
        ),
        in_specs=[anywhere, anywhere],
        out_specs=(anywhere, anywhere),
        scratch_shapes=[pltpu.SemaphoreType.DMA((3,))] * 4,
        compiler_params=pltpu.CompilerParams(collective_id=1, has_side_effects=True),
        name="exchange",
    )(send, slots)


def collect_kernel(slot_ref, rslot_ref, me_ref, own_ref, recv_ref, out_ref, acc, flipped):
    me = me_ref[0]

    @pl.loop(0, OSLOT)
    def _(b):
        acc[b] = jnp.zeros((32, 128), jnp.float32)

    @pl.loop(0, CAP)
    def _(p):
        b = slot_ref[me * CAP + p]
        acc[b] = acc[b] + own_ref[p]

    for j in range(3):
        @pl.loop(0, CAP)
        def _(p):
            b = rslot_ref[j * POS + me * CAP + p]
            acc[b] = acc[b] + recv_ref[j, p].astype(jnp.float32)

    lane = lax.broadcasted_iota(jnp.int32, (32, 128), 1)
    low = lane < 64
    even = lax.rem(lane // 32, 2) == 0

    @pl.loop(0, OSLOT // 8)
    def _(g):
        for quad in range(2):
            block = acc[pl.ds(g * 8 + quad * 4, 4)].reshape(128, 128)
            flipped[quad] = block.T
            parts = [
                flipped[quad, pl.ds(half * 64 + parity, 32, stride=2), :]
                for parity in range(2) for half in range(2)
            ]
            mid = [None] * 4
            for n in range(2):
                a, b = parts[n], parts[n + 2]
                mid[n] = jnp.where(low, a, pltpu.roll(b, 64, 1))
                mid[n + 2] = jnp.where(low, pltpu.roll(a, 64, 1), b)
            for n in range(2):
                a, b = mid[2 * n], mid[2 * n + 1]
                first = jnp.where(even, a, pltpu.roll(b, 32, 1))
                second = jnp.where(even, pltpu.roll(a, 96, 1), b)
                for which, value in ((2 * n, first), (2 * n + 1, second)):
                    out_ref[pl.ds(g * 256 + quad * 4 + which, 32, stride=8), :] = value


def collect(slots, rslots, me, own, recv):
    smem = pl.BlockSpec(memory_space=pltpu.SMEM)
    vmem = pl.BlockSpec(memory_space=pltpu.VMEM)
    return pl.pallas_call(
        collect_kernel,
        out_shape=jax.ShapeDtypeStruct((OSLOT * 32, 128), jnp.float32),
        in_specs=[smem, smem, smem, vmem, vmem],
        out_specs=vmem,
        scratch_shapes=[pltpu.VMEM((OSLOT, 32, 128), jnp.float32), pltpu.VMEM((2, 128, 128), jnp.float32)],
        compiler_params=pltpu.CompilerParams(vmem_limit_bytes=32 * 1024 * 1024),
        name="collect",
    )(slots, rslots, me, own, recv)


NBLK = 64
STEPS = (0, 1, -1, 2)
PIECES = [
    (layer, first, turn, along, across)
    for layer in (0, 1) for first in (0, 1) for turn in (0, 1) for along in STEPS for across in STEPS
]
PIECE_ID = {piece: number for number, piece in enumerate(PIECES)}


def next_hops(piece):
    layer, first, turn, along, across = piece
    dims = ("x", "y") if first == 0 else ("y", "x")
    sign = 1 - 2 * turn
    hops = []
    if across == 0:
        if along == 0:
            hops += [(dims[0], sign, (layer, first, turn, 1, 0)), (dims[0], -sign, (layer, first, turn, -1, 0))]
        if along == 1:
            hops += [(dims[0], sign, (layer, first, turn, 2, 0))]
        hops += [(dims[1], sign, (layer, first, turn, along, 1)), (dims[1], -sign, (layer, first, turn, along, -1))]
    elif across == 1:
        hops += [(dims[1], sign, (layer, first, turn, along, 2))]
    return hops


def arrival_order(slot=1.46, latency=2.0, far_slot=5.8, far_latency=4.0, issue=0.05):
    heap, order, free, clock, count = [], [], {}, 0.0, 0
    for layer in (0, 1):
        for number, (first, turn) in enumerate(((0, 0), (0, 1), (1, 0), (1, 1))):
            when = 0.0 if layer == 0 else (number + 1) * far_slot + far_latency
            heapq.heappush(heap, (when, 0, count, (layer, first, turn, 0, 0)))
            count += 1
    while heap:
        when, _, _, piece = heapq.heappop(heap)
        clock = max(clock, when)
        order.append(piece)
        for dim, sign, after in next_hops(piece):
            clock += issue
            free[dim, sign] = max(clock, free.get((dim, sign), 0.0)) + slot
            heapq.heappush(heap, (free[dim, sign] + latency, -len(next_hops(after)), count, after))
            count += 1
        clock += issue
    return order


def gather_kernel(own_ref, panel_ref, send_sem, recv_sems, near_send, near_recv, own_sem):
    blk, grp = lax.axis_index("blk"), lax.axis_index("grp")
    core = lax.rem(blk, 2)
    x = lax.rem(blk // 2, 4)
    y = lax.rem(blk // 8, 4)
    high = blk // 32
    where = {"x": x, "y": y}

    def number(high, y, x, core):
        return ((high * 4 + y) * 4 + x) * 2 + core

    def moved(dim, by):
        at = dict(where)
        at[dim] = lax.rem(at[dim] + by + 4, 4)
        return number(high, at["y"], at["x"], core)

    sibling = number(high, y, x, 1 - core)
    opposite = number(1 - high, y, x, core)
    neighbours = {(dim, sign): moved(dim, sign) for dim in ("x", "y") for sign in (1, -1)}

    barrier = pltpu.get_barrier_semaphore()
    for other in (sibling, opposite, *neighbours.values()):
        pl.semaphore_signal(barrier, inc=1, device_id=(other, grp), device_id_type=MESH)
    pl.semaphore_wait(barrier, 6)

    def origin(piece):
        layer, first, turn, along, across = piece
        sign = 1 - 2 * turn
        dims = ("x", "y") if first == 0 else ("y", "x")
        at = dict(where)
        at[dims[0]] = lax.rem(at[dims[0]] - sign * along + 4, 4)
        at[dims[1]] = lax.rem(at[dims[1]] - sign * across + 4, 4)
        return number(high if layer == 0 else 1 - high, at["y"], at["x"], core)

    def rows(piece):
        return pl.ds(2 * (2 * piece[1] + piece[2]), 2)

    def remote(src, dst, sems, target):
        return pltpu.make_async_remote_copy(
            src_ref=src, dst_ref=dst, send_sem=sems[0], recv_sem=sems[1], device_id=(target, grp), device_id_type=MESH)

    def held(piece):
        return panel_ref.at[origin(piece), rows(piece)]

    mine = pltpu.make_async_copy(own_ref, panel_ref.at[blk], own_sem.at[0])
    for piece in ORDER[:4]:
        for dim, sign, after in next_hops(piece):
            remote(own_ref.at[rows(piece)], held(piece), (send_sem.at[0], recv_sems.at[PIECE_ID[after]]),
                   neighbours[dim, sign]).start()
        far = (1,) + piece[1:]
        remote(own_ref.at[rows(piece)], held(piece), (send_sem.at[0], recv_sems.at[PIECE_ID[far]]), opposite).start()
    remote(own_ref, panel_ref.at[blk], (near_send.at[0], near_recv.at[0]), sibling).start()
    mine.start()
    for piece in ORDER[4:]:
        here = held(piece)
        remote(here, here, (send_sem.at[0], recv_sems.at[PIECE_ID[piece]]), sibling).wait_recv()
        for dim, sign, after in next_hops(piece):
            remote(here, here, (send_sem.at[0], recv_sems.at[PIECE_ID[after]]), neighbours[dim, sign]).start()
        remote(here, here, (near_send.at[0], near_recv.at[0]), sibling).start()
    mine.wait()
    most = panel_ref.at[pl.ds(0, 31)]
    pltpu.make_async_copy(most, most, send_sem.at[0]).wait()
    half = panel_ref.at[pl.ds(0, 32)]
    pltpu.make_async_copy(half, half, near_send.at[0]).wait()
    pltpu.make_async_copy(half, half, near_recv.at[0]).wait()


ORDER = arrival_order()


def gather(own):
    anywhere = pl.BlockSpec(memory_space=pl.ANY)
    return pl.pallas_call(
        gather_kernel,
        out_shape=jax.ShapeDtypeStruct((NBLK, RF, 128, 128), jnp.bfloat16),
        in_specs=[anywhere],
        out_specs=anywhere,
        scratch_shapes=[
            pltpu.SemaphoreType.DMA((1,)),
            pltpu.SemaphoreType.DMA((len(PIECES),)),
            pltpu.SemaphoreType.DMA((1,)),
            pltpu.SemaphoreType.DMA((1,)),
            pltpu.SemaphoreType.DMA((1,)),
        ],
        compiler_params=pltpu.CompilerParams(collective_id=0, has_side_effects=True),
        name="gather",
    )(own)


def arranged(p_tiles):
    return p_tiles.reshape(RF, TILE, KP, 2, 32).transpose(0, 2, 4, 3, 1).reshape(RF, 128, 128)


def body(a_tiles, a_cols, p_tiles, route_list, out_slot):
    me = lax.axis_index("grp").astype(jnp.int32).reshape(1)
    cols = a_cols.reshape(SLOTS)
    cols = cols // (RF * GRP) * RF + cols % RF
    panel = gather(arranged(p_tiles)).reshape(NBLK * RF, 128, 128)
    send, own = product(cols, route_list.reshape(RF * 256), me, a_tiles, p_tiles, panel)
    slots = out_slot.reshape(2, 128)
    recv, rslots = exchange(send, slots)
    out = collect(slots.reshape(POS), rslots.reshape(3 * POS), me, own, recv)
    return out.reshape(16, 32, 8, 128).transpose(0, 2, 1, 3).reshape(OSLOT, TILE * TILE)


def solution(mesh):
    in_specs = (
        P(("blk", "grp"), None, None),
        P(("blk", "grp"), None),
        P(("blk", "grp"), None, None),
        P(("blk", "grp"), None),
        P(("blk", "grp"), None),
    )
    out_specs = P(("blk", "grp"), None)
    return jax.shard_map(body, mesh=mesh, in_specs=in_specs, out_specs=out_specs, check_vma=False)
```

```python
import heapq

import jax
import jax.numpy as jnp
from jax import lax
from jax.experimental import pallas as pl
from jax.experimental.pallas import tpu as pltpu
from jax.sharding import PartitionSpec as P

TILE = 64
RF = 8
KA = 16
KP = 4
CAP = 64
OSLOT = 128
GRP = 4
SLOTS = RF * KA
POS = GRP * CAP
MESH = pl.DeviceIdType.MESH
NACC = 4
LOW = 16
ROWS = KP * LOW
YUN = 8
WUN = 8


def low_lanes(shape):
    return lax.broadcasted_iota(jnp.int32, shape, 1) < TILE


def turned(block):
    return pltpu.roll(block.astype(jnp.float32), TILE, 1).astype(jnp.bfloat16)


def product_kernel(cols_ref, route_ref, me_ref, tiles_ref, p_ref, panel_ref, send_ref, own_ref, weights, ys, a_ref, a_sem,
                   *accs):
    fetch = pltpu.make_async_copy(tiles_ref, a_ref, a_sem.at[0])
    fetch.start()
    low = low_lanes((TILE, 128))
    zero = jnp.zeros((TILE, 128), jnp.bfloat16)

    @pl.loop(0, RF)
    def _(i):
        for half in range(2):
            pair = p_ref[i, :, half * 128:(half + 1) * 128]
            back = turned(pair)
            even, odd = 2 * half * 128, (2 * half + 1) * 128
            weights[i, 0:TILE, even:even + 128] = jnp.where(low, pair, zero)
            weights[i, TILE:128, even:even + 128] = jnp.where(low, zero, back)
            weights[i, 0:TILE, odd:odd + 128] = jnp.where(low, back, zero)
            weights[i, TILE:128, odd:odd + 128] = jnp.where(low, zero, pair)

    @pl.loop(0, POS // 4)
    def _(r):
        for acc in accs:
            acc[pl.ds(pl.multiple_of(r * 4 * LOW, 8), 4 * LOW), :] = jnp.zeros((4 * LOW, 128), jnp.float32)

    fetch.wait()

    @pl.loop(0, RF)
    def _(i):
        @pl.loop(0, KA // YUN)
        def _(kk):
            for u in range(YUN // 2):
                pair = a_ref[i, :, pl.ds(pl.multiple_of(kk * (64 * YUN) + u * 128, 128), 128)]
                back = turned(pair)
                for parity in range(2):
                    first, second = (pair, back) if parity == 0 else (back, pair)
                    tile = jnp.concatenate([jnp.where(low, first, zero), jnp.where(low, zero, second)], axis=0)
                    m = i * KA + kk * YUN + 2 * u + parity
                    ys[m] = lax.dot_general(
                        panel_ref[cols_ref[m]], tile, (((1,), (1,)), ((), ())), preferred_element_type=jnp.float32
                    ).astype(jnp.bfloat16)

    @pl.loop(0, SLOTS // WUN)
    def _(step):
        i = step // (KA // WUN)
        k0 = lax.rem(step, KA // WUN) * WUN
        base = i * 256 + k0 * KP
        y = ys[pl.ds(step * WUN, WUN)].reshape(WUN * ROWS, 128)
        w = [
            jnp.dot(y, weights[i, :, sp * 256:(sp + 1) * 256], preferred_element_type=jnp.float32)
            for sp in range(2)
        ]
        for u in range(WUN):
            for q in range(KP):
                for s in range(KP):
                    r = route_ref[base + (s * KA + u) * KP + q]
                    acc = accs[s % NACC]
                    row, lane = u * ROWS + q * LOW, s % 2 * 128
                    here = pl.ds(pl.multiple_of(r, LOW), LOW)
                    acc[here, :] = acc[here, :] + w[s // 2][row:row + LOW, lane:lane + 128]

    def total(r, count):
        here = pl.ds(pl.multiple_of(r * LOW, LOW), count * LOW)
        value = (accs[0][here, :] + accs[1][here, :]) + (accs[2][here, :] + accs[3][here, :])
        return value.reshape(count, LOW, 128)

    @pl.loop(0, POS // 4)
    def _(step):
        send_ref[pl.ds(step * 4, 4)] = total(step * 4, 4).astype(jnp.bfloat16)

    @pl.loop(0, CAP // 4)
    def _(step):
        own_ref[pl.ds(step * 4, 4)] = total(me_ref[0] * CAP + step * 4, 4)


def product(cols, route, me, a_tiles, p_tiles, panel):
    smem = pl.BlockSpec(memory_space=pltpu.SMEM)
    vmem = pl.BlockSpec(memory_space=pltpu.VMEM)
    return pl.pallas_call(
        product_kernel,
        out_shape=(
            jax.ShapeDtypeStruct((POS, LOW, 128), jnp.bfloat16),
            jax.ShapeDtypeStruct((CAP, LOW, 128), jnp.float32),
        ),
        in_specs=[smem, smem, smem, pl.BlockSpec(memory_space=pltpu.HBM), vmem, vmem],
        out_specs=(vmem, vmem),
        scratch_shapes=[
            pltpu.VMEM((RF, 128, 512), jnp.bfloat16),
            pltpu.VMEM((SLOTS, ROWS, 128), jnp.bfloat16),
            pltpu.VMEM((RF, TILE, KA * TILE), jnp.bfloat16),
            pltpu.SemaphoreType.DMA((1,)),
        ]
        + [pltpu.VMEM((POS * LOW, 128), jnp.float32)] * NACC,
        compiler_params=pltpu.CompilerParams(vmem_limit_bytes=16 * 1024 * 1024),
        name="product",
    )(cols, route, me, a_tiles, p_tiles, panel)


def collect_kernel(slot_ref, rslot_ref, me_ref, own0_ref, own1_ref, recv0_ref, recv1_ref, out_ref, *scratch):
    accs, flipped = scratch[:4], scratch[4]
    me = me_ref[0]

    @pl.loop(0, OSLOT // 2)
    def _(b):
        for acc in accs:
            acc[pl.ds(b * 2, 2)] = jnp.zeros((2, 32, 128), jnp.float32)

    @pl.loop(0, CAP // 2)
    def _(step):
        for e in range(2):
            p = step * 2 + e
            for j in range(4):
                b = slot_ref[me * CAP + p] if j == 3 else rslot_ref[j * POS + me * CAP + p]
                low = own0_ref[p] if j == 3 else recv0_ref[j, p].astype(jnp.float32)
                high = own1_ref[p] if j == 3 else recv1_ref[j, p].astype(jnp.float32)
                accs[j][b, 0:LOW] = accs[j][b, 0:LOW] + low
                accs[j][b, LOW:] = accs[j][b, LOW:] + high

    lane = lax.broadcasted_iota(jnp.int32, (32, 128), 1)
    low = lane < 64
    even = lax.rem(lane // 32, 2) == 0

    @pl.loop(0, OSLOT // 8)
    def _(g):
        for quad in range(2):
            here = pl.ds(g * 8 + quad * 4, 4)
            block = ((accs[0][here] + accs[1][here]) + (accs[2][here] + accs[3][here])).reshape(128, 128)
            flipped[quad] = block.T
            parts = [
                flipped[quad, pl.ds(half * 64 + parity, 32, stride=2), :]
                for parity in range(2) for half in range(2)
            ]
            mid = [None] * 4
            for n in range(2):
                a, b = parts[n], parts[n + 2]
                mid[n] = jnp.where(low, a, pltpu.roll(b, 64, 1))
                mid[n + 2] = jnp.where(low, pltpu.roll(a, 64, 1), b)
            for n in range(2):
                a, b = mid[2 * n], mid[2 * n + 1]
                first = jnp.where(even, a, pltpu.roll(b, 32, 1))
                second = jnp.where(even, pltpu.roll(a, 96, 1), b)
                for which, value in ((2 * n, first), (2 * n + 1, second)):
                    out_ref[pl.ds(g * 256 + quad * 4 + which, 32, stride=8), :] = value


def collect(slots, rslots, me, own0, own1, recv0, recv1):
    smem = pl.BlockSpec(memory_space=pltpu.SMEM)
    vmem = pl.BlockSpec(memory_space=pltpu.VMEM)
    return pl.pallas_call(
        collect_kernel,
        out_shape=jax.ShapeDtypeStruct((OSLOT * 32, 128), jnp.float32),
        in_specs=[smem, smem, smem, vmem, vmem, vmem, vmem],
        out_specs=vmem,
        scratch_shapes=[pltpu.VMEM((OSLOT, 32, 128), jnp.float32)] * 4 + [pltpu.VMEM((2, 128, 128), jnp.float32)],
        compiler_params=pltpu.CompilerParams(vmem_limit_bytes=16 * 1024 * 1024),
        name="collect",
    )(slots, rslots, me, own0, own1, recv0, recv1)


NBLK = 64
STEPS = (0, 1, -1, 2)
PIECES = [
    (layer, first, turn, along, across)
    for layer in (0, 1) for first in (0, 1) for turn in (0, 1) for along in STEPS for across in STEPS
]
PIECE_ID = {piece: number for number, piece in enumerate(PIECES)}


def next_hops(piece):
    layer, first, turn, along, across = piece
    dims = ("x", "y") if first == 0 else ("y", "x")
    sign = 1 - 2 * turn
    hops = []
    if across == 0:
        if along == 0:
            hops += [(dims[0], sign, (layer, first, turn, 1, 0)), (dims[0], -sign, (layer, first, turn, -1, 0))]
        if along == 1:
            hops += [(dims[0], sign, (layer, first, turn, 2, 0))]
        hops += [(dims[1], sign, (layer, first, turn, along, 1)), (dims[1], -sign, (layer, first, turn, along, -1))]
    elif across == 1:
        hops += [(dims[1], sign, (layer, first, turn, along, 2))]
    return hops


def arrival_order(slot=1.46, latency=2.0, far_slot=5.8, far_latency=4.0, issue=0.05):
    heap, order, free, clock, count = [], [], {}, 0.0, 0
    for layer in (0, 1):
        for number, (first, turn) in enumerate(((0, 0), (0, 1), (1, 0), (1, 1))):
            when = 0.0 if layer == 0 else (number + 1) * far_slot + far_latency
            heapq.heappush(heap, (when, 0, count, (layer, first, turn, 0, 0)))
            count += 1
    while heap:
        when, _, _, piece = heapq.heappop(heap)
        clock = max(clock, when)
        order.append(piece)
        for dim, sign, after in next_hops(piece):
            clock += issue
            free[dim, sign] = max(clock, free.get((dim, sign), 0.0)) + slot
            heapq.heappush(heap, (free[dim, sign] + latency, -len(next_hops(after)), count, after))
            count += 1
        clock += issue
    return order


def remote(src, dst, send_sem, recv_sem, target):
    return pltpu.make_async_remote_copy(
        src_ref=src, dst_ref=dst, send_sem=send_sem, recv_sem=recv_sem, device_id=target, device_id_type=MESH)


def partners():
    blk, me = lax.axis_index("blk"), lax.axis_index("grp")
    return {1: (blk, me + 1 - 2 * lax.rem(me, 2)), 2: (blk, lax.rem(me + 2, 4)), 3: (blk, 3 - me)}


class Place:
    def __init__(self):
        self.blk, self.grp = lax.axis_index("blk"), lax.axis_index("grp")
        self.core = lax.rem(self.blk, 2)
        self.at = {"x": lax.rem(self.blk // 2, 4), "y": lax.rem(self.blk // 8, 4)}
        self.high = self.blk // 32
        self.sibling = (self.number(self.high, self.at, 1 - self.core), self.grp)
        self.far = self.number(1 - self.high, self.at, self.core)
        self.opposite = (self.far, self.grp)
        self.neighbours = {
            (dim, sign): (self.moved(dim, sign), self.grp) for dim in ("x", "y") for sign in (1, -1)
        }

    def number(self, high, at, core):
        return ((high * 4 + at["y"]) * 4 + at["x"]) * 2 + core

    def moved(self, dim, by):
        at = dict(self.at)
        at[dim] = lax.rem(at[dim] + by + 4, 4)
        return self.number(self.high, at, self.core)

    def origin(self, piece):
        layer, first, turn, along, across = piece
        sign = 1 - 2 * turn
        dims = ("x", "y") if first == 0 else ("y", "x")
        at = dict(self.at)
        at[dims[0]] = lax.rem(at[dims[0]] - sign * along + 4, 4)
        at[dims[1]] = lax.rem(at[dims[1]] - sign * across + 4, 4)
        return self.number(self.high if layer == 0 else 1 - self.high, at, self.core)


def greet(targets):
    barrier = pltpu.get_barrier_semaphore()
    for target in targets:
        pl.semaphore_signal(barrier, inc=1, device_id=target, device_id_type=MESH)
    pl.semaphore_wait(barrier, len(targets))


def rows(piece):
    return pl.ds(2 * (2 * piece[1] + piece[2]), 2)


def settle(ref, count, sem):
    part = ref.at[pl.ds(0, count)]
    pltpu.make_async_copy(part, part, sem).wait()


def spread(place, panel_ref, order, start, sems, between):
    send_sem, recv_sems, near_send, near_recv = sems

    def held(piece):
        return panel_ref.at[place.origin(piece), rows(piece)]

    for piece in start:
        source = start[piece]
        for dim, sign, after in next_hops(piece):
            remote(source, held(piece), send_sem.at[0], recv_sems.at[PIECE_ID[after]], place.neighbours[dim, sign]).start()
    count = 0
    for piece in order:
        if piece in start:
            continue
        if count in between:
            between[count]()
        count += 1
        here = held(piece)
        remote(here, here, send_sem.at[0], recv_sems.at[PIECE_ID[piece]], place.sibling).wait_recv()
        for dim, sign, after in next_hops(piece):
            remote(here, here, send_sem.at[0], recv_sems.at[PIECE_ID[after]], place.neighbours[dim, sign]).start()
        remote(here, here, near_send.at[0], near_recv.at[0], place.sibling).start()


ORIGINS = [(first, turn, 0, 0) for first, turn in ((0, 0), (0, 1), (1, 0), (1, 1))]


def gather_kernel(own_ref, panel_ref, later_ref, send_sem, recv_sems, near_send, near_recv, first_sems, later_sems,
                  own_sem, transit, later_transit):
    place = Place()
    z = place.high * 4 + place.grp

    def above(by):
        level = lax.rem(z + by + 8, 8)
        return place.number(level // 4, place.at, place.core), lax.rem(level, 4)

    greet([place.sibling, above(1), above(-1), above(3), above(-3), *place.neighbours.values()])
    start = {(0,) + piece: own_ref.at[0, rows((0,) + piece)] for piece in ORIGINS}
    sems = (send_sem, recv_sems, near_send, near_recv)
    lates = []

    def first_leg():
        for number, piece in enumerate(start):
            remote(start[piece], transit.at[number], send_sem.at[0], first_sems.at[number],
                   above(1 - 2 * piece[2])).start()
        for turn in range(2):
            part = pl.ds(4 * turn, 4)
            lates.append(remote(own_ref.at[1, part], later_transit.at[turn], later_sems.at[turn], later_sems.at[2 + turn],
                                above(1 - 2 * turn)))
            lates[-1].start()
        remote(own_ref.at[0], panel_ref.at[place.blk], near_send.at[0], near_recv.at[0], place.sibling).start()
        pltpu.make_async_copy(own_ref.at[0], panel_ref.at[place.blk], own_sem.at[0]).start()
        for number, piece in enumerate(start):
            up = 1 - 2 * piece[2]
            remote(transit.at[number], transit.at[number], send_sem.at[0], first_sems.at[number], above(up)).wait_recv()
            remote(transit.at[number], panel_ref.at[above(-up)[0], rows(piece)], send_sem.at[0],
                   recv_sems.at[PIECE_ID[(1,) + piece[1:]]], above(3 * up)).start()

    def second_leg():
        for turn in range(2):
            lates[turn].wait_recv()
            lates.append(remote(later_transit.at[turn], later_ref.at[pl.ds(4 * turn, 4)], later_sems.at[4 + turn],
                                later_sems.at[6 + turn], above(3 * (1 - 2 * turn))))
            lates[-1].start()

    spread(place, panel_ref, ORDER_A, start, sems, {0: first_leg, 24: second_leg})
    pltpu.make_async_copy(own_ref.at[0], panel_ref.at[place.blk], own_sem.at[0]).wait()
    for turn in range(2):
        lates[turn].wait_send()
        lates[2 + turn].wait()
    settle(panel_ref, 32, send_sem.at[0])
    settle(panel_ref, 32, near_send.at[0])
    settle(panel_ref, 32, near_recv.at[0])


def swap(send_ref, recv_ref, sems):
    send_sems, recv_sems = sems
    copies = []
    for j, target in reversed(partners().items()):
        copies.append(remote(
            send_ref.at[pl.ds(target[1] * CAP, CAP)], recv_ref.at[j - 1], send_sems.at[j - 1], recv_sems.at[j - 1],
            target))
        copies[-1].start()
    return copies


def gather_swap_kernel(own_ref, later_ref, send_ref, slot_ref, panel_ref, recv_ref, rslot_ref, send_sem, recv_sems,
                       near_send, near_recv, own_sems, swap_send, swap_recv, slot_send, slot_recv):
    place = Place()
    greet([place.sibling, *place.neighbours.values(), *partners().values()])
    copies = swap(send_ref, recv_ref, (swap_send, swap_recv))
    start = {(0,) + piece: own_ref.at[1, rows((0,) + piece)] for piece in ORIGINS}
    start |= {(1,) + piece: later_ref.at[rows((1,) + piece)] for piece in ORIGINS}
    mine = []

    def rest():
        for number, (source, slot) in enumerate(((own_ref.at[1], place.blk), (later_ref, place.far))):
            remote(source, panel_ref.at[slot], near_send.at[0], near_recv.at[0], place.sibling).start()
            mine.append(pltpu.make_async_copy(source, panel_ref.at[slot], own_sems.at[number]))
            mine[-1].start()
        for j, target in partners().items():
            copies.append(remote(slot_ref, rslot_ref.at[j - 1], slot_send.at[j - 1], slot_recv.at[j - 1], target))
            copies[-1].start()

    spread(place, panel_ref, ORDER_B, start, (send_sem, recv_sems, near_send, near_recv), {0: rest})
    for copy in mine:
        copy.wait()
    settle(panel_ref, 30, send_sem.at[0])
    settle(panel_ref, 32, near_send.at[0])
    settle(panel_ref, 32, near_recv.at[0])
    for copy in copies:
        copy.wait()


def swap_kernel(send_ref, recv_ref, swap_send, swap_recv):
    greet(list(partners().values()))
    for copy in swap(send_ref, recv_ref, (swap_send, swap_recv)):
        copy.wait()


ORDER_A = arrival_order(slot=0.73, far_slot=1.5, far_latency=5.0)
ORDER_B = arrival_order(slot=0.73, far_slot=0.0, far_latency=0.0)
ANYWHERE = pl.BlockSpec(memory_space=pl.ANY)
PANEL = jax.ShapeDtypeStruct((NBLK, RF, ROWS, 128), jnp.bfloat16)
RECV = jax.ShapeDtypeStruct((3, CAP, LOW, 128), jnp.bfloat16)
ONE = pltpu.SemaphoreType.DMA((1,))
TWO = pltpu.SemaphoreType.DMA((2,))
THREE = pltpu.SemaphoreType.DMA((3,))
MANY = pltpu.SemaphoreType.DMA((len(PIECES),))


def gather(own):
    return pl.pallas_call(
        gather_kernel,
        out_shape=(PANEL, jax.ShapeDtypeStruct((RF, ROWS, 128), jnp.bfloat16)),
        in_specs=[ANYWHERE],
        out_specs=(ANYWHERE, ANYWHERE),
        scratch_shapes=[
            ONE, MANY, ONE, ONE, pltpu.SemaphoreType.DMA((4,)), pltpu.SemaphoreType.DMA((8,)), ONE,
            pltpu.VMEM((4, 2, ROWS, 128), jnp.bfloat16),
            pltpu.VMEM((2, 4, ROWS, 128), jnp.bfloat16),
        ],
        compiler_params=pltpu.CompilerParams(collective_id=0, has_side_effects=True, vmem_limit_bytes=1 << 20),
        cost_estimate=pl.CostEstimate(flops=0, transcendentals=0, bytes_accessed=1 << 26),
        name="gather",
    )(own)


def gather_swap(own, later, send, slots):
    return pl.pallas_call(
        gather_swap_kernel,
        out_shape=(PANEL, RECV, jax.ShapeDtypeStruct((3, 2, 128), jnp.int32)),
        in_specs=[ANYWHERE] * 4,
        out_specs=(ANYWHERE, ANYWHERE, ANYWHERE),
        scratch_shapes=[ONE, MANY, ONE, ONE, TWO, THREE, THREE, THREE, THREE],
        compiler_params=pltpu.CompilerParams(collective_id=1, has_side_effects=True, vmem_limit_bytes=1 << 20),
        cost_estimate=pl.CostEstimate(flops=0, transcendentals=0, bytes_accessed=1 << 26),
        name="gather_swap",
    )(own, later, send, slots)


def exchange(send):
    return pl.pallas_call(
        swap_kernel,
        out_shape=RECV,
        in_specs=[ANYWHERE],
        out_specs=ANYWHERE,
        scratch_shapes=[THREE, THREE],
        compiler_params=pltpu.CompilerParams(collective_id=2, has_side_effects=True, vmem_limit_bytes=1 << 20),
        name="exchange",
    )(send)


def arrange_kernel(p_ref, out_ref):
    group = lax.broadcasted_iota(jnp.int32, (TILE, 128), 1) // 32

    def merged(parts):
        value = parts[0]
        for number in (1, 2, 3):
            value = jnp.where(group == number, parts[number], value)
        return value

    @pl.loop(0, RF)
    def _(i):
        left = p_ref[i, :, 0:128].astype(jnp.float32)
        right = p_ref[i, :, 128:256].astype(jnp.float32)
        first = merged([left, pltpu.roll(left, 96, 1), pltpu.roll(right, 64, 1), pltpu.roll(right, 32, 1)])
        second = merged([pltpu.roll(left, 96, 1), pltpu.roll(left, 64, 1), pltpu.roll(right, 32, 1), right])
        block = jnp.concatenate([first, second], axis=0).T.astype(jnp.bfloat16)
        for q in range(KP):
            for part in range(2):
                out_ref[part, i, q * LOW:(q + 1) * LOW, :] = block[q * 32 + part * LOW:q * 32 + (part + 1) * LOW]


def arranged(p_tiles):
    vmem = pl.BlockSpec(memory_space=pltpu.VMEM)
    return pl.pallas_call(
        arrange_kernel,
        out_shape=jax.ShapeDtypeStruct((2, RF, ROWS, 128), jnp.bfloat16),
        in_specs=[vmem],
        out_specs=vmem,
        compiler_params=pltpu.CompilerParams(vmem_limit_bytes=4 * 1024 * 1024),
        name="arrange",
    )(p_tiles)


def body(a_tiles, a_cols, p_tiles, route_list, out_slot):
    me = lax.axis_index("grp").astype(jnp.int32).reshape(1)
    cols = a_cols.reshape(SLOTS)
    cols = cols // (RF * GRP) * RF + cols % RF
    route = route_list.reshape(RF * 256) * LOW
    slots = out_slot.reshape(2, 128)
    arranged_tiles = arranged(p_tiles)
    panel0, later = gather(arranged_tiles)
    send0, own0 = product(cols, route, me, a_tiles, p_tiles, panel0.reshape(NBLK * RF, ROWS, 128))
    panel1, recv0, rslots = gather_swap(arranged_tiles, later, send0, slots)
    send1, own1 = product(cols, route, me, a_tiles, p_tiles, panel1.reshape(NBLK * RF, ROWS, 128))
    recv1 = exchange(send1)
    out = collect(slots.reshape(POS), rslots.reshape(3 * POS), me, own0, own1, recv0, recv1)
    return out.reshape(16, 32, 8, 128).transpose(0, 2, 1, 3).reshape(OSLOT, TILE * TILE)


def solution(mesh):
    in_specs = (
        P(("blk", "grp"), None, None),
        P(("blk", "grp"), None),
        P(("blk", "grp"), None, None),
        P(("blk", "grp"), None),
        P(("blk", "grp"), None),
    )
    out_specs = P(("blk", "grp"), None)
    return jax.shard_map(body, mesh=mesh, in_specs=in_specs, out_specs=out_specs, check_vma=False)
```

```python
import functools
import heapq

import jax
import jax.numpy as jnp
from jax import lax
from jax.experimental import pallas as pl
from jax.experimental.pallas import tpu as pltpu
from jax.sharding import PartitionSpec as P

TILE = 64
RF = 8
KA = 16
KP = 4
CAP = 64
OSLOT = 128
GRP = 4
SLOTS = RF * KA
POS = GRP * CAP
MESH = pl.DeviceIdType.MESH
NACC = 4
LOW = 16
ROWS = KP * LOW
WUN = 16


def low_lanes(shape):
    return lax.broadcasted_iota(jnp.int32, shape, 1) < TILE


def turned(block):
    return pltpu.roll(block.astype(jnp.float32), TILE, 1).astype(jnp.bfloat16)


def build_weights(p_ref, weights):
    low = low_lanes((TILE, 128))
    zero = jnp.zeros((TILE, 128), jnp.bfloat16)

    @pl.loop(0, RF)
    def _(i):
        for half in range(2):
            pair = p_ref[i, :, half * 128:(half + 1) * 128]
            back = turned(pair)
            even, odd = 2 * half * 128, (2 * half + 1) * 128
            weights[i, 0:TILE, even:even + 128] = jnp.where(low, pair, zero)
            weights[i, TILE:128, even:even + 128] = jnp.where(low, zero, back)
            weights[i, 0:TILE, odd:odd + 128] = jnp.where(low, back, zero)
            weights[i, TILE:128, odd:odd + 128] = jnp.where(low, zero, pair)


def build_tiles(a_ref, tiles_ref, i):
    low = low_lanes((TILE, 128))
    zero = jnp.zeros((TILE, 128), jnp.bfloat16)

    @pl.loop(0, KA // 2)
    def _(kk):
        pair = a_ref[i, :, pl.ds(pl.multiple_of(kk * 128, 128), 128)]
        back = turned(pair)
        for parity in range(2):
            first, second = (pair, back) if parity == 0 else (back, pair)
            m = i * KA + kk * 2 + parity
            tiles_ref[m, 0:TILE, :] = jnp.where(low, first, zero)
            tiles_ref[m, TILE:128, :] = jnp.where(low, zero, second)


def product_kernel(cols_ref, route_ref, me_ref, tiles_ref, weights, panel_ref, blank0, blank1, blank2, blank3, send_ref,
                   own_ref, acc0, acc1, acc2, acc3, ys):
    accs = (acc0, acc1, acc2, acc3)

    @pl.loop(0, RF)
    def _(i):
        for k in range(KA):
            m = i * KA + k
            col = cols_ref[i, k]
            ys[m] = lax.dot_general(
                panel_ref[(col >> 5) * RF + (col & 7)], tiles_ref[m], (((1,), (1,)), ((), ())), preferred_element_type=jnp.float32
            ).astype(jnp.bfloat16)

    @pl.loop(0, SLOTS // WUN)
    def _(step):
        i = step // (KA // WUN)
        k0 = lax.rem(step, KA // WUN) * WUN
        base = i * 256 + k0 * KP
        y = ys[pl.ds(step * WUN, WUN)].reshape(WUN * ROWS, 128)
        w = [
            jnp.dot(y, weights[i, :, sp * 256:(sp + 1) * 256], preferred_element_type=jnp.float32)
            for sp in range(2)
        ]
        for u in range(WUN):
            for q in range(KP):
                for s in range(KP):
                    r = route_ref[base + (s * KA + u) * KP + q]
                    acc = accs[s % NACC]
                    row, lane = u * ROWS + q * LOW, s % 2 * 128
                    here = pl.ds(pl.multiple_of(r, LOW), LOW)
                    acc[here, :] = acc[here, :] + w[s // 2][row:row + LOW, lane:lane + 128]

    def total(r, count):
        here = pl.ds(pl.multiple_of(r * LOW, LOW), count * LOW)
        value = (accs[0][here, :] + accs[1][here, :]) + (accs[2][here, :] + accs[3][here, :])
        return value.reshape(count, LOW, 128)

    @pl.loop(0, POS // 4)
    def _(step):
        send_ref[pl.ds(step * 4, 4)] = total(step * 4, 4).astype(jnp.bfloat16)

    @pl.loop(0, CAP // 4)
    def _(step):
        own_ref[pl.ds(step * 4, 4)] = total(me_ref[0] * CAP + step * 4, 4)


def product(cols, route, me, tiles, weights, panel, blanks):
    smem = pl.BlockSpec(memory_space=pltpu.SMEM)
    vmem = pl.BlockSpec(memory_space=pltpu.VMEM)
    return pl.pallas_call(
        product_kernel,
        out_shape=(
            jax.ShapeDtypeStruct((POS, LOW, 128), jnp.bfloat16),
            jax.ShapeDtypeStruct((CAP, LOW, 128), jnp.float32),
            *[BLANK] * NACC,
        ),
        in_specs=[smem, smem, smem, vmem, vmem, vmem, *[vmem] * NACC],
        out_specs=(vmem, vmem, *[vmem] * NACC),
        scratch_shapes=[pltpu.VMEM((SLOTS, ROWS, 128), jnp.bfloat16)],
        input_output_aliases={6 + n: 2 + n for n in range(NACC)},
        compiler_params=pltpu.CompilerParams(vmem_limit_bytes=16 * 1024 * 1024),
        name="product",
    )(cols, route, me, tiles, weights, panel, *blanks)[:2]


def collect_kernel(slot_ref, rslot_ref, me_ref, own0_ref, own1_ref, recv0_ref, recv1_ref, out_ref, *scratch):
    accs, flipped = scratch[:4], scratch[4]
    me = me_ref[0]

    @pl.loop(0, OSLOT // 2)
    def _(b):
        for acc in accs:
            acc[pl.ds(b * 2, 2)] = jnp.zeros((2, 32, 128), jnp.float32)

    @pl.loop(0, CAP // 2)
    def _(step):
        for e in range(2):
            p = step * 2 + e
            for j in range(4):
                b = slot_ref[me * CAP + p] if j == 3 else rslot_ref[j * POS + me * CAP + p]
                low = own0_ref[p] if j == 3 else recv0_ref[j, p].astype(jnp.float32)
                high = own1_ref[p] if j == 3 else recv1_ref[j, p].astype(jnp.float32)
                accs[j][b, 0:LOW] = accs[j][b, 0:LOW] + low
                accs[j][b, LOW:] = accs[j][b, LOW:] + high

    lane = lax.broadcasted_iota(jnp.int32, (32, 128), 1)
    low = lane < 64
    even = lax.rem(lane // 32, 2) == 0

    @pl.loop(0, OSLOT // 16)
    def _(g):
        quads = range(4)
        for quad in quads:
            here = pl.ds(g * 16 + quad * 4, 4)
            block = ((accs[0][here] + accs[1][here]) + (accs[2][here] + accs[3][here])).reshape(128, 128)
            flipped[quad] = block.T
        for quad in quads:
            parts = [
                flipped[quad, pl.ds(half * 64 + parity, 32, stride=2), :]
                for parity in range(2) for half in range(2)
            ]
            mid = [None] * 4
            for n in range(2):
                a, b = parts[n], parts[n + 2]
                mid[n] = jnp.where(low, a, pltpu.roll(b, 64, 1))
                mid[n + 2] = jnp.where(low, pltpu.roll(a, 64, 1), b)
            for n in range(2):
                a, b = mid[2 * n], mid[2 * n + 1]
                first = jnp.where(even, a, pltpu.roll(b, 32, 1))
                second = jnp.where(even, pltpu.roll(a, 96, 1), b)
                for which, value in ((2 * n, first), (2 * n + 1, second)):
                    row = g * 512 + quad // 2 * 256 + quad % 2 * 4 + which
                    out_ref[pl.ds(row, 32, stride=8), :] = value


def collect(slots, rslots, me, own0, own1, recv0, recv1):
    smem = pl.BlockSpec(memory_space=pltpu.SMEM)
    vmem = pl.BlockSpec(memory_space=pltpu.VMEM)
    return pl.pallas_call(
        collect_kernel,
        out_shape=jax.ShapeDtypeStruct((OSLOT * 32, 128), jnp.float32),
        in_specs=[smem, smem, smem, vmem, vmem, vmem, vmem],
        out_specs=vmem,
        scratch_shapes=[pltpu.VMEM((OSLOT, 32, 128), jnp.float32)] * 4 + [pltpu.VMEM((4, 128, 128), jnp.float32)],
        compiler_params=pltpu.CompilerParams(vmem_limit_bytes=16 * 1024 * 1024),
        name="collect",
    )(slots, rslots, me, own0, own1, recv0, recv1)


NBLK = 64
STEPS = (0, 1, -1, 2)
PIECES = [
    (layer, first, turn, along, across)
    for layer in (0, 1) for first in (0, 1) for turn in (0, 1) for along in STEPS for across in STEPS
]
PIECE_ID = {piece: number for number, piece in enumerate(PIECES)}


def next_hops(piece):
    layer, first, turn, along, across = piece
    dims = ("x", "y") if first == 0 else ("y", "x")
    sign = 1 - 2 * turn
    hops = []
    if across == 0:
        if along == 0:
            hops += [(dims[0], sign, (layer, first, turn, 1, 0)), (dims[0], -sign, (layer, first, turn, -1, 0))]
        if along == 1:
            hops += [(dims[0], sign, (layer, first, turn, 2, 0))]
        hops += [(dims[1], sign, (layer, first, turn, along, 1)), (dims[1], -sign, (layer, first, turn, along, -1))]
    elif across == 1:
        hops += [(dims[1], sign, (layer, first, turn, along, 2))]
    return hops


def arrival_order(slot=1.46, latency=2.0, far_slot=5.8, far_latency=4.0, issue=0.05):
    heap, order, free, clock, count = [], [], {}, 0.0, 0
    for layer in (0, 1):
        for number, (first, turn) in enumerate(((0, 0), (0, 1), (1, 0), (1, 1))):
            when = 0.0 if layer == 0 else (number + 1) * far_slot + far_latency
            heapq.heappush(heap, (when, 0, count, (layer, first, turn, 0, 0)))
            count += 1
    while heap:
        when, _, _, piece = heapq.heappop(heap)
        clock = max(clock, when)
        order.append(piece)
        for dim, sign, after in next_hops(piece):
            clock += issue
            free[dim, sign] = max(clock, free.get((dim, sign), 0.0)) + slot
            heapq.heappush(heap, (free[dim, sign] + latency, -len(next_hops(after)), count, after))
            count += 1
        clock += issue
    return order


def remote(src, dst, send_sem, recv_sem, target):
    return pltpu.make_async_remote_copy(
        src_ref=src, dst_ref=dst, send_sem=send_sem, recv_sem=recv_sem, device_id=target, device_id_type=MESH)


def partners():
    blk, me = lax.axis_index("blk"), lax.axis_index("grp")
    return {1: (blk, me + 1 - 2 * lax.rem(me, 2)), 2: (blk, lax.rem(me + 2, 4)), 3: (blk, 3 - me)}


class Place:
    def __init__(self):
        self.blk, self.grp = lax.axis_index("blk"), lax.axis_index("grp")
        self.core = lax.rem(self.blk, 2)
        self.at = {"x": lax.rem(self.blk // 2, 4), "y": lax.rem(self.blk // 8, 4)}
        self.high = self.blk // 32
        self.sibling = (self.number(self.high, self.at, 1 - self.core), self.grp)
        self.far = self.number(1 - self.high, self.at, self.core)
        self.opposite = (self.far, self.grp)
        self.neighbours = {
            (dim, sign): (self.moved(dim, sign), self.grp) for dim in ("x", "y") for sign in (1, -1)
        }

    def number(self, high, at, core):
        return ((high * 4 + at["y"]) * 4 + at["x"]) * 2 + core

    def moved(self, dim, by):
        at = dict(self.at)
        at[dim] = lax.rem(at[dim] + by + 4, 4)
        return self.number(self.high, at, self.core)

    def origin(self, piece):
        layer, first, turn, along, across = piece
        sign = 1 - 2 * turn
        dims = ("x", "y") if first == 0 else ("y", "x")
        at = dict(self.at)
        at[dims[0]] = lax.rem(at[dims[0]] - sign * along + 4, 4)
        at[dims[1]] = lax.rem(at[dims[1]] - sign * across + 4, 4)
        return self.number(self.high if layer == 0 else 1 - self.high, at, self.core)


def greet(targets):
    barrier = pltpu.get_barrier_semaphore()
    for target in targets:
        pl.semaphore_signal(barrier, inc=1, device_id=target, device_id_type=MESH)
    pl.semaphore_wait(barrier, len(targets))


def rows(piece):
    return pl.ds(2 * (2 * piece[1] + piece[2]), 2)


def settle(ref, count, sem):
    part = ref.at[pl.ds(0, count)]
    pltpu.make_async_copy(part, part, sem).wait()


def spread(place, panel_ref, order, start, sems, between):
    send_sem, recv_sems, near_send, near_recv = sems

    def held(piece):
        return panel_ref.at[place.origin(piece), rows(piece)]

    for piece in start:
        source = start[piece]
        for dim, sign, after in next_hops(piece):
            remote(source, held(piece), send_sem.at[0], recv_sems.at[PIECE_ID[after]], place.neighbours[dim, sign]).start()
    count = 0
    for piece in order:
        if piece in start:
            continue
        if count in between:
            between[count]()
        count += 1
        here = held(piece)
        remote(here, here, send_sem.at[0], recv_sems.at[PIECE_ID[piece]], place.sibling).wait_recv()
        for dim, sign, after in next_hops(piece):
            remote(here, here, send_sem.at[0], recv_sems.at[PIECE_ID[after]], place.neighbours[dim, sign]).start()
        remote(here, here, near_send.at[0], near_recv.at[0], place.sibling).start()


ORIGINS = [(first, turn, 0, 0) for first, turn in ((0, 0), (0, 1), (1, 0), (1, 1))]


def clear(ref):
    @pl.loop(0, POS * LOW // 64)
    def _(step):
        ref[pl.ds(pl.multiple_of(step * 64, 64), 64), :] = jnp.zeros((64, 128), jnp.float32)


def gather_kernel(own_ref, a_hbm, panel_ref, later_ref, tiles_ref, blank0, blank1, blank2, blank3, send_sem, recv_sems, near_send,
                  near_recv, first_sems, later_sems, own_sem, a_sem, transit, later_transit, a_ref):
    place = Place()
    z = place.high * 4 + place.grp

    def above(by):
        level = lax.rem(z + by + 8, 8)
        return place.number(level // 4, place.at, place.core), lax.rem(level, 4)

    fetch = pltpu.make_async_copy(a_hbm, a_ref, a_sem.at[0])
    fetch.start()
    greet([place.sibling, above(1), above(-1), above(3), above(-3), *place.neighbours.values()])
    start = {(0,) + piece: own_ref.at[0, rows((0,) + piece)] for piece in ORIGINS}
    sems = (send_sem, recv_sems, near_send, near_recv)
    for number, piece in enumerate(start):
        remote(start[piece], transit.at[number], send_sem.at[0], first_sems.at[number], above(1 - 2 * piece[2])).start()
    lates = []

    def first_leg():
        remote(own_ref.at[0], panel_ref.at[place.blk], near_send.at[0], near_recv.at[0], place.sibling).start()
        pltpu.make_async_copy(own_ref.at[0], panel_ref.at[place.blk], own_sem.at[0]).start()
        for number, piece in enumerate(start):
            up = 1 - 2 * piece[2]
            remote(transit.at[number], transit.at[number], send_sem.at[0], first_sems.at[number], above(up)).wait_recv()
            remote(transit.at[number], panel_ref.at[above(-up)[0], rows(piece)], send_sem.at[0],
                   recv_sems.at[PIECE_ID[(1,) + piece[1:]]], above(3 * up)).start()
        for turn in range(2):
            part = pl.ds(4 * turn, 4)
            lates.append(remote(own_ref.at[1, part], later_transit.at[turn], later_sems.at[turn], later_sems.at[2 + turn],
                                above(1 - 2 * turn)))
            lates[-1].start()

    def second_leg():
        for turn in range(2):
            lates[turn].wait_recv()
            lates.append(remote(later_transit.at[turn], later_ref.at[pl.ds(4 * turn, 4)], later_sems.at[4 + turn],
                                later_sems.at[6 + turn], above(3 * (1 - 2 * turn))))
            lates[-1].start()

    between = {0: first_leg, 30: second_leg, 40: fetch.wait}
    for i in range(RF):
        between[44 + 8 * i] = functools.partial(build_tiles, a_ref, tiles_ref, i)
    for n, blank in enumerate((blank0, blank1, blank2, blank3)):
        between[50 + 16 * n] = functools.partial(clear, blank)
    spread(place, panel_ref, ORDER_A, start, sems, between)
    pltpu.make_async_copy(own_ref.at[0], panel_ref.at[place.blk], own_sem.at[0]).wait()
    for turn in range(2):
        lates[turn].wait_send()
        lates[2 + turn].wait()
    settle(panel_ref, 32, send_sem.at[0])
    settle(panel_ref, 32, near_send.at[0])
    settle(panel_ref, 32, near_recv.at[0])


def swap(send_ref, recv_ref, sems):
    send_sems, recv_sems = sems
    copies = []
    for j, target in reversed(partners().items()):
        copies.append(remote(
            send_ref.at[pl.ds(target[1] * CAP, CAP)], recv_ref.at[j - 1], send_sems.at[j - 1], recv_sems.at[j - 1],
            target))
        copies[-1].start()
    return copies


def gather_swap_kernel(own_ref, later_ref, send_ref, slot_ref, panel_ref, recv_ref, rslot_ref, blank0, blank1, blank2,
                       blank3, send_sem, recv_sems,
                       near_send, near_recv, own_sems, swap_send, swap_recv, slot_send, slot_recv):
    place = Place()
    greet([place.sibling, *place.neighbours.values(), *partners().values()])
    copies = swap(send_ref, recv_ref, (swap_send, swap_recv))
    start = {(0,) + piece: own_ref.at[1, rows((0,) + piece)] for piece in ORIGINS}
    start |= {(1,) + piece: later_ref.at[rows((1,) + piece)] for piece in ORIGINS}
    mine = []

    def rest():
        for number, (source, slot) in enumerate(((own_ref.at[1], place.blk), (later_ref, place.far))):
            remote(source, panel_ref.at[slot], near_send.at[0], near_recv.at[0], place.sibling).start()
            mine.append(pltpu.make_async_copy(source, panel_ref.at[slot], own_sems.at[number]))
            mine[-1].start()
        for j, target in partners().items():
            copies.append(remote(slot_ref, rslot_ref.at[j - 1], slot_send.at[j - 1], slot_recv.at[j - 1], target))
            copies[-1].start()

    between = {0: rest}
    for n, blank in enumerate((blank0, blank1, blank2, blank3)):
        between[30 + 20 * n] = functools.partial(clear, blank)
    spread(place, panel_ref, ORDER_B, start, (send_sem, recv_sems, near_send, near_recv), between)
    for copy in mine:
        copy.wait()
    settle(panel_ref, 30, send_sem.at[0])
    settle(panel_ref, 32, near_send.at[0])
    settle(panel_ref, 32, near_recv.at[0])
    for copy in copies:
        copy.wait()


def swap_kernel(send_ref, recv_ref, swap_send, swap_recv):
    greet(list(partners().values()))
    for copy in swap(send_ref, recv_ref, (swap_send, swap_recv)):
        copy.wait()


ORDER_A = arrival_order(slot=0.73, latency=3.0, far_slot=1.5, far_latency=5.0)
ORDER_B = arrival_order(slot=0.73, far_slot=0.0, far_latency=0.0)
ANYWHERE = pl.BlockSpec(memory_space=pl.ANY)
PANEL = jax.ShapeDtypeStruct((NBLK, RF, ROWS, 128), jnp.bfloat16)
BLANK = jax.ShapeDtypeStruct((POS * LOW, 128), jnp.float32)
GATHER_VMEM = 12 << 20
RECV = jax.ShapeDtypeStruct((3, CAP, LOW, 128), jnp.bfloat16)
ONE = pltpu.SemaphoreType.DMA((1,))
TWO = pltpu.SemaphoreType.DMA((2,))
THREE = pltpu.SemaphoreType.DMA((3,))
MANY = pltpu.SemaphoreType.DMA((len(PIECES),))


def gather(own, a_tiles):
    vmem = pl.BlockSpec(memory_space=pltpu.VMEM)
    return pl.pallas_call(
        gather_kernel,
        out_shape=(
            PANEL,
            jax.ShapeDtypeStruct((RF, ROWS, 128), jnp.bfloat16),
            jax.ShapeDtypeStruct((SLOTS, 128, 128), jnp.bfloat16),
            *[BLANK] * NACC,
        ),
        in_specs=[ANYWHERE, pl.BlockSpec(memory_space=pltpu.HBM)],
        out_specs=(ANYWHERE, ANYWHERE, vmem, *[vmem] * NACC),
        scratch_shapes=[
            ONE, MANY, ONE, ONE, pltpu.SemaphoreType.DMA((4,)), pltpu.SemaphoreType.DMA((8,)), ONE, ONE,
            pltpu.VMEM((4, 2, ROWS, 128), jnp.bfloat16),
            pltpu.VMEM((2, 4, ROWS, 128), jnp.bfloat16),
            pltpu.VMEM((RF, TILE, KA * TILE), jnp.bfloat16),
        ],
        compiler_params=pltpu.CompilerParams(collective_id=0, has_side_effects=True, vmem_limit_bytes=GATHER_VMEM),
        cost_estimate=pl.CostEstimate(flops=0, transcendentals=0, bytes_accessed=1 << 26),
        name="gather",
    )(own, a_tiles)


def gather_swap(own, later, send, slots):
    vmem = pl.BlockSpec(memory_space=pltpu.VMEM)
    return pl.pallas_call(
        gather_swap_kernel,
        out_shape=(PANEL, RECV, jax.ShapeDtypeStruct((3, 2, 128), jnp.int32), *[BLANK] * NACC),
        in_specs=[ANYWHERE] * 4,
        out_specs=(ANYWHERE, ANYWHERE, ANYWHERE, *[vmem] * NACC),
        scratch_shapes=[ONE, MANY, ONE, ONE, TWO, THREE, THREE, THREE, THREE],
        compiler_params=pltpu.CompilerParams(collective_id=1, has_side_effects=True, vmem_limit_bytes=12 << 20),
        cost_estimate=pl.CostEstimate(flops=0, transcendentals=0, bytes_accessed=1 << 26),
        name="gather_swap",
    )(own, later, send, slots)


def exchange(send):
    return pl.pallas_call(
        swap_kernel,
        out_shape=RECV,
        in_specs=[ANYWHERE],
        out_specs=ANYWHERE,
        scratch_shapes=[THREE, THREE],
        compiler_params=pltpu.CompilerParams(collective_id=2, has_side_effects=True, vmem_limit_bytes=1 << 20),
        name="exchange",
    )(send)


def arrange_kernel(p_ref, route_ref, out_ref, line_ref, weights_ref):
    build_weights(p_ref, weights_ref)
    for half in range(2):
        line_ref[pl.ds(half, RF, stride=2), :] = route_ref[:, half * 128:(half + 1) * 128] * LOW
    group = lax.broadcasted_iota(jnp.int32, (TILE, 128), 1) // 32

    def merged(parts):
        value = parts[0]
        for number in (1, 2, 3):
            value = jnp.where(group == number, parts[number], value)
        return value

    @pl.loop(0, RF)
    def _(i):
        left = p_ref[i, :, 0:128].astype(jnp.float32)
        right = p_ref[i, :, 128:256].astype(jnp.float32)
        first = merged([left, pltpu.roll(left, 96, 1), pltpu.roll(right, 64, 1), pltpu.roll(right, 32, 1)])
        second = merged([pltpu.roll(left, 96, 1), pltpu.roll(left, 64, 1), pltpu.roll(right, 32, 1), right])
        block = jnp.concatenate([first, second], axis=0).T.astype(jnp.bfloat16)
        for q in range(KP):
            for part in range(2):
                out_ref[part, i, q * LOW:(q + 1) * LOW, :] = block[q * 32 + part * LOW:q * 32 + (part + 1) * LOW]


def arranged(p_tiles, route_list):
    vmem = pl.BlockSpec(memory_space=pltpu.VMEM)
    return pl.pallas_call(
        arrange_kernel,
        out_shape=(
            jax.ShapeDtypeStruct((2, RF, ROWS, 128), jnp.bfloat16),
            jax.ShapeDtypeStruct((2 * RF, 128), jnp.int32),
            jax.ShapeDtypeStruct((RF, 128, 512), jnp.bfloat16),
        ),
        in_specs=[vmem, vmem],
        out_specs=(vmem, vmem, vmem),
        compiler_params=pltpu.CompilerParams(vmem_limit_bytes=4 * 1024 * 1024),
        name="arrange",
    )(p_tiles, route_list)


def body(a_tiles, a_cols, p_tiles, route_list, out_slot):
    me = lax.axis_index("grp").astype(jnp.int32).reshape(1)
    slots = out_slot.reshape(2, 128)
    arranged_tiles, route, weights = arranged(p_tiles, route_list)
    route = route.reshape(RF * 256)
    panel0, later, tiles, *blank0 = gather(arranged_tiles, a_tiles)
    send0, own0 = product(a_cols, route, me, tiles, weights, panel0.reshape(NBLK * RF, ROWS, 128), blank0)
    panel1, recv0, rslots, *blank1 = gather_swap(arranged_tiles, later, send0, slots)
    send1, own1 = product(a_cols, route, me, tiles, weights, panel1.reshape(NBLK * RF, ROWS, 128), blank1)
    recv1 = exchange(send1)
    out = collect(slots.reshape(POS), rslots.reshape(3 * POS), me, own0, own1, recv0, recv1)
    return out.reshape(16, 32, 8, 128).transpose(0, 2, 1, 3).reshape(OSLOT, TILE * TILE)


def solution(mesh):
    in_specs = (
        P(("blk", "grp"), None, None),
        P(("blk", "grp"), None),
        P(("blk", "grp"), None, None),
        P(("blk", "grp"), None),
        P(("blk", "grp"), None),
    )
    out_specs = P(("blk", "grp"), None)
    return jax.shard_map(body, mesh=mesh, in_specs=in_specs, out_specs=out_specs, check_vma=False)
```

```python
import functools
import heapq

import jax
import jax.numpy as jnp
from jax import lax
from jax.experimental import pallas as pl
from jax.experimental.pallas import tpu as pltpu
from jax.sharding import PartitionSpec as P

TILE = 64
RF = 8
KA = 16
KP = 4
CAP = 64
OSLOT = 128
GRP = 4
SLOTS = RF * KA
POS = GRP * CAP
MESH = pl.DeviceIdType.MESH
NACC = 4
LOW = 16
ROWS = KP * LOW
WUN = 16


def low_lanes(shape):
    return lax.broadcasted_iota(jnp.int32, shape, 1) < TILE


def turned(block):
    return pltpu.roll(block.astype(jnp.float32), TILE, 1).astype(jnp.bfloat16)


def build_weights(p_ref, weights):
    low = low_lanes((TILE, 128))
    zero = jnp.zeros((TILE, 128), jnp.bfloat16)

    @pl.loop(0, RF)
    def _(i):
        for half in range(2):
            pair = p_ref[i, :, half * 128:(half + 1) * 128]
            back = turned(pair)
            even, odd = 2 * half * 128, (2 * half + 1) * 128
            weights[i, 0:TILE, even:even + 128] = jnp.where(low, pair, zero)
            weights[i, TILE:128, even:even + 128] = jnp.where(low, zero, back)
            weights[i, 0:TILE, odd:odd + 128] = jnp.where(low, back, zero)
            weights[i, TILE:128, odd:odd + 128] = jnp.where(low, zero, pair)


def build_tiles(a_ref, tiles_ref, i):
    low = low_lanes((TILE, 128))
    zero = jnp.zeros((TILE, 128), jnp.bfloat16)

    @pl.loop(0, KA // 2)
    def _(kk):
        pair = a_ref[i, :, pl.ds(pl.multiple_of(kk * 128, 128), 128)]
        back = turned(pair)
        for parity in range(2):
            first, second = (pair, back) if parity == 0 else (back, pair)
            m = i * KA + kk * 2 + parity
            tiles_ref[m, 0:TILE, :] = jnp.where(low, first, zero)
            tiles_ref[m, TILE:128, :] = jnp.where(low, zero, second)


def product_kernel(lines_ref, me_ref, tiles_ref, weights, panel_ref, blank0, blank1, blank2, blank3, send_ref,
                   own_ref, acc0, acc1, acc2, acc3, ys):
    accs = (acc0, acc1, acc2, acc3)

    @pl.loop(0, RF)
    def _(i):
        for k in range(KA):
            m = i * KA + k
            col = lines_ref[2 * RF * 128 + i * 128 + k]
            ys[m] = lax.dot_general(
                panel_ref[(col >> 5) * RF + (col & 7)], tiles_ref[m], (((1,), (1,)), ((), ())), preferred_element_type=jnp.float32
            ).astype(jnp.bfloat16)

    @pl.loop(0, SLOTS // WUN)
    def _(step):
        i = step // (KA // WUN)
        k0 = lax.rem(step, KA // WUN) * WUN
        base = i * 256 + k0 * KP
        y = ys[pl.ds(step * WUN, WUN)].reshape(WUN * ROWS, 128)
        w = [
            jnp.dot(y, weights[i, :, sp * 256:(sp + 1) * 256], preferred_element_type=jnp.float32)
            for sp in range(2)
        ]
        for u in range(WUN):
            for q in range(KP):
                for s in range(KP):
                    r = lines_ref[base + (s * KA + u) * KP + q]
                    acc = accs[s % NACC]
                    row, lane = u * ROWS + q * LOW, s % 2 * 128
                    here = pl.ds(pl.multiple_of(r, LOW), LOW)
                    acc[here, :] = acc[here, :] + w[s // 2][row:row + LOW, lane:lane + 128]

    def total(r, count):
        here = pl.ds(pl.multiple_of(r * LOW, LOW), count * LOW)
        value = (accs[0][here, :] + accs[1][here, :]) + (accs[2][here, :] + accs[3][here, :])
        return value.reshape(count, LOW, 128)

    @pl.loop(0, POS // 4)
    def _(step):
        send_ref[pl.ds(step * 4, 4)] = total(step * 4, 4).astype(jnp.bfloat16)

    @pl.loop(0, CAP // 4)
    def _(step):
        own_ref[pl.ds(step * 4, 4)] = total(me_ref[0] * CAP + step * 4, 4)


def product(lines, me, tiles, weights, panel, blanks):
    smem = pl.BlockSpec(memory_space=pltpu.SMEM)
    vmem = pl.BlockSpec(memory_space=pltpu.VMEM)
    return pl.pallas_call(
        product_kernel,
        out_shape=(
            jax.ShapeDtypeStruct((POS, LOW, 128), jnp.bfloat16),
            jax.ShapeDtypeStruct((CAP, LOW, 128), jnp.float32),
            *[BLANK] * NACC,
        ),
        in_specs=[smem, smem, vmem, vmem, vmem, *[vmem] * NACC],
        out_specs=(vmem, vmem, *[vmem] * NACC),
        scratch_shapes=[pltpu.VMEM((SLOTS, ROWS, 128), jnp.bfloat16)],
        input_output_aliases={5 + n: 2 + n for n in range(NACC)},
        compiler_params=pltpu.CompilerParams(vmem_limit_bytes=16 * 1024 * 1024),
        name="product",
    )(lines, me, tiles, weights, panel, *blanks)[:2]


def collect_kernel(slot_ref, rslot_ref, me_ref, own0_ref, own1_ref, recv0_ref, recv1_ref, blank0, blank1, blank2, blank3,
                   out_ref, acc0, acc1, acc2, acc3, flipped):
    accs = (acc0, acc1, acc2, acc3)
    me = me_ref[0]

    @pl.loop(0, CAP // 2)
    def _(step):
        for e in range(2):
            p = step * 2 + e
            for j in range(4):
                b = slot_ref[me * CAP + p] if j == 3 else rslot_ref[j * POS + me * CAP + p]
                low = own0_ref[p] if j == 3 else recv0_ref[j, p].astype(jnp.float32)
                high = own1_ref[p] if j == 3 else recv1_ref[j, p].astype(jnp.float32)
                here = pl.ds(pl.multiple_of(b * 32, 32), LOW)
                there = pl.ds(pl.multiple_of(b * 32 + LOW, LOW), LOW)
                accs[j][here, :] = accs[j][here, :] + low
                accs[j][there, :] = accs[j][there, :] + high

    lane = lax.broadcasted_iota(jnp.int32, (32, 128), 1)
    low = lane < 64
    even = lax.rem(lane // 32, 2) == 0

    @pl.loop(0, OSLOT // 16)
    def _(g):
        quads = range(4)
        for quad in quads:
            here = pl.ds(pl.multiple_of(g * 512 + quad * 128, 128), 128)
            block = (accs[0][here, :] + accs[1][here, :]) + (accs[2][here, :] + accs[3][here, :])
            flipped[quad] = block.T
        for quad in quads:
            parts = [
                flipped[quad, pl.ds(half * 64 + parity, 32, stride=2), :]
                for parity in range(2) for half in range(2)
            ]
            mid = [None] * 4
            for n in range(2):
                a, b = parts[n], parts[n + 2]
                mid[n] = jnp.where(low, a, pltpu.roll(b, 64, 1))
                mid[n + 2] = jnp.where(low, pltpu.roll(a, 64, 1), b)
            for n in range(2):
                a, b = mid[2 * n], mid[2 * n + 1]
                first = jnp.where(even, a, pltpu.roll(b, 32, 1))
                second = jnp.where(even, pltpu.roll(a, 96, 1), b)
                for which, value in ((2 * n, first), (2 * n + 1, second)):
                    row = g * 512 + quad // 2 * 256 + quad % 2 * 4 + which
                    out_ref[pl.ds(row, 32, stride=8), :] = value


def collect(slots, rslots, me, own0, own1, recv0, recv1, blanks):
    smem = pl.BlockSpec(memory_space=pltpu.SMEM)
    vmem = pl.BlockSpec(memory_space=pltpu.VMEM)
    return pl.pallas_call(
        collect_kernel,
        out_shape=(jax.ShapeDtypeStruct((OSLOT * 32, 128), jnp.float32), *[BLANK] * 4),
        in_specs=[smem, smem, smem, vmem, vmem, vmem, vmem, *[vmem] * 4],
        out_specs=(vmem, *[vmem] * 4),
        scratch_shapes=[pltpu.VMEM((4, 128, 128), jnp.float32)],
        input_output_aliases={7 + n: 1 + n for n in range(4)},
        compiler_params=pltpu.CompilerParams(vmem_limit_bytes=16 * 1024 * 1024),
        name="collect",
    )(slots, rslots, me, own0, own1, recv0, recv1, *blanks)[0]


NBLK = 64
STEPS = (0, 1, -1, 2)
PIECES = [
    (layer, first, turn, along, across)
    for layer in (0, 1) for first in (0, 1) for turn in (0, 1) for along in STEPS for across in STEPS
]
PIECE_ID = {piece: number for number, piece in enumerate(PIECES)}


def next_hops(piece):
    layer, first, turn, along, across = piece
    dims = ("x", "y") if first == 0 else ("y", "x")
    sign = 1 - 2 * turn
    hops = []
    if across == 0:
        if along == 0:
            hops += [(dims[0], sign, (layer, first, turn, 1, 0)), (dims[0], -sign, (layer, first, turn, -1, 0))]
        if along == 1:
            hops += [(dims[0], sign, (layer, first, turn, 2, 0))]
        hops += [(dims[1], sign, (layer, first, turn, along, 1)), (dims[1], -sign, (layer, first, turn, along, -1))]
    elif across == 1:
        hops += [(dims[1], sign, (layer, first, turn, along, 2))]
    return hops


def arrival_order(slot=1.46, latency=2.0, far_slot=5.8, far_latency=4.0, issue=0.05):
    heap, order, free, clock, count = [], [], {}, 0.0, 0
    for layer in (0, 1):
        for number, (first, turn) in enumerate(((0, 0), (0, 1), (1, 0), (1, 1))):
            when = 0.0 if layer == 0 else (number + 1) * far_slot + far_latency
            heapq.heappush(heap, (when, 0, count, (layer, first, turn, 0, 0)))
            count += 1
    while heap:
        when, _, _, piece = heapq.heappop(heap)
        clock = max(clock, when)
        order.append(piece)
        for dim, sign, after in next_hops(piece):
            clock += issue
            free[dim, sign] = max(clock, free.get((dim, sign), 0.0)) + slot
            heapq.heappush(heap, (free[dim, sign] + latency, -len(next_hops(after)), count, after))
            count += 1
        clock += issue
    return order


def remote(src, dst, send_sem, recv_sem, target):
    return pltpu.make_async_remote_copy(
        src_ref=src, dst_ref=dst, send_sem=send_sem, recv_sem=recv_sem, device_id=target, device_id_type=MESH)


def partners():
    blk, me = lax.axis_index("blk"), lax.axis_index("grp")
    return {1: (blk, me + 1 - 2 * lax.rem(me, 2)), 2: (blk, lax.rem(me + 2, 4)), 3: (blk, 3 - me)}


class Place:
    def __init__(self):
        self.blk, self.grp = lax.axis_index("blk"), lax.axis_index("grp")
        self.core = lax.rem(self.blk, 2)
        self.at = {"x": lax.rem(self.blk // 2, 4), "y": lax.rem(self.blk // 8, 4)}
        self.high = self.blk // 32
        self.sibling = (self.number(self.high, self.at, 1 - self.core), self.grp)
        self.far = self.number(1 - self.high, self.at, self.core)
        self.opposite = (self.far, self.grp)
        self.neighbours = {
            (dim, sign): (self.moved(dim, sign), self.grp) for dim in ("x", "y") for sign in (1, -1)
        }

    def number(self, high, at, core):
        return ((high * 4 + at["y"]) * 4 + at["x"]) * 2 + core

    def moved(self, dim, by):
        at = dict(self.at)
        at[dim] = lax.rem(at[dim] + by + 4, 4)
        return self.number(self.high, at, self.core)

    def origin(self, piece):
        layer, first, turn, along, across = piece
        sign = 1 - 2 * turn
        dims = ("x", "y") if first == 0 else ("y", "x")
        at = dict(self.at)
        at[dims[0]] = lax.rem(at[dims[0]] - sign * along + 4, 4)
        at[dims[1]] = lax.rem(at[dims[1]] - sign * across + 4, 4)
        return self.number(self.high if layer == 0 else 1 - self.high, at, self.core)


def greet(targets):
    barrier = pltpu.get_barrier_semaphore()
    for target in targets:
        pl.semaphore_signal(barrier, inc=1, device_id=target, device_id_type=MESH)
    pl.semaphore_wait(barrier, len(targets))


def rows(piece):
    return pl.ds(2 * (2 * piece[1] + piece[2]), 2)


def settle(ref, count, sem):
    part = ref.at[pl.ds(0, count)]
    pltpu.make_async_copy(part, part, sem).wait()


def spread(place, panel_ref, order, start, sems, between):
    send_sem, recv_sems, near_send, near_recv = sems

    def held(piece):
        return panel_ref.at[place.origin(piece), rows(piece)]

    for piece in start:
        source = start[piece]
        for dim, sign, after in next_hops(piece):
            remote(source, held(piece), send_sem.at[0], recv_sems.at[PIECE_ID[after]], place.neighbours[dim, sign]).start()
    count = 0
    for piece in order:
        if piece in start:
            continue
        if count in between:
            between[count]()
        count += 1
        here = held(piece)
        remote(here, here, send_sem.at[0], recv_sems.at[PIECE_ID[piece]], place.sibling).wait_recv()
        for dim, sign, after in next_hops(piece):
            remote(here, here, send_sem.at[0], recv_sems.at[PIECE_ID[after]], place.neighbours[dim, sign]).start()
        remote(here, here, near_send.at[0], near_recv.at[0], place.sibling).start()


ORIGINS = [(first, turn, 0, 0) for first, turn in ((0, 0), (0, 1), (1, 0), (1, 1))]


def clear(ref):
    @pl.loop(0, POS * LOW // 64)
    def _(step):
        ref[pl.ds(pl.multiple_of(step * 64, 64), 64), :] = jnp.zeros((64, 128), jnp.float32)


def gather_kernel(own_ref, a_hbm, p_hbm, panel_ref, later_ref, tiles_ref, weights_ref, blank0, blank1, blank2, blank3, send_sem, recv_sems, near_send,
                  near_recv, first_sems, later_sems, own_sem, a_sem, transit, later_transit, a_ref, p_ref):
    place = Place()
    z = place.high * 4 + place.grp

    def above(by):
        level = lax.rem(z + by + 8, 8)
        return place.number(level // 4, place.at, place.core), lax.rem(level, 4)

    fetch = pltpu.make_async_copy(a_hbm, a_ref, a_sem.at[0])
    fetch.start()
    fetch_p = pltpu.make_async_copy(p_hbm, p_ref, a_sem.at[1])
    fetch_p.start()
    greet([place.sibling, above(1), above(-1), above(3), above(-3), *place.neighbours.values()])
    start = {(0,) + piece: own_ref.at[0, rows((0,) + piece)] for piece in ORIGINS}
    sems = (send_sem, recv_sems, near_send, near_recv)
    for number, piece in enumerate(start):
        remote(start[piece], transit.at[number], send_sem.at[0], first_sems.at[number], above(1 - 2 * piece[2])).start()
    lates = []

    def first_leg():
        remote(own_ref.at[0], panel_ref.at[place.blk], near_send.at[0], near_recv.at[0], place.sibling).start()
        pltpu.make_async_copy(own_ref.at[0], panel_ref.at[place.blk], own_sem.at[0]).start()
        for number, piece in enumerate(start):
            up = 1 - 2 * piece[2]
            remote(transit.at[number], transit.at[number], send_sem.at[0], first_sems.at[number], above(up)).wait_recv()
            remote(transit.at[number], panel_ref.at[above(-up)[0], rows(piece)], send_sem.at[0],
                   recv_sems.at[PIECE_ID[(1,) + piece[1:]]], above(3 * up)).start()
        for turn in range(2):
            part = pl.ds(4 * turn, 4)
            lates.append(remote(own_ref.at[1, part], later_transit.at[turn], later_sems.at[turn], later_sems.at[2 + turn],
                                above(1 - 2 * turn)))
            lates[-1].start()

    def second_leg():
        for turn in range(2):
            lates[turn].wait_recv()
            lates.append(remote(later_transit.at[turn], later_ref.at[pl.ds(4 * turn, 4)], later_sems.at[4 + turn],
                                later_sems.at[6 + turn], above(3 * (1 - 2 * turn))))
            lates[-1].start()

    between = {0: first_leg, 30: second_leg, 40: fetch.wait}

    def weights():
        fetch_p.wait()
        build_weights(p_ref, weights_ref)

    between[36] = weights
    for i in range(RF):
        between[44 + 8 * i] = functools.partial(build_tiles, a_ref, tiles_ref, i)
    for n, blank in enumerate((blank0, blank1, blank2, blank3)):
        between[50 + 16 * n] = functools.partial(clear, blank)
    spread(place, panel_ref, ORDER_A, start, sems, between)
    pltpu.make_async_copy(own_ref.at[0], panel_ref.at[place.blk], own_sem.at[0]).wait()
    for turn in range(2):
        lates[turn].wait_send()
        lates[2 + turn].wait()
    settle(panel_ref, 32, send_sem.at[0])
    settle(panel_ref, 32, near_send.at[0])
    settle(panel_ref, 32, near_recv.at[0])


def swap(send_ref, recv_ref, sems):
    send_sems, recv_sems = sems
    copies = []
    for j, target in reversed(partners().items()):
        copies.append(remote(
            send_ref.at[pl.ds(target[1] * CAP, CAP)], recv_ref.at[j - 1], send_sems.at[j - 1], recv_sems.at[j - 1],
            target))
        copies[-1].start()
    return copies


def gather_swap_kernel(own_ref, later_ref, send_ref, slot_ref, panel_ref, recv_ref, rslot_ref, blank0, blank1, blank2,
                       blank3, send_sem, recv_sems,
                       near_send, near_recv, own_sems, swap_send, swap_recv, slot_send, slot_recv):
    place = Place()
    greet([place.sibling, *place.neighbours.values(), *partners().values()])
    copies = swap(send_ref, recv_ref, (swap_send, swap_recv))
    start = {(0,) + piece: own_ref.at[1, rows((0,) + piece)] for piece in ORIGINS}
    start |= {(1,) + piece: later_ref.at[rows((1,) + piece)] for piece in ORIGINS}
    mine = []

    def rest():
        for number, (source, slot) in enumerate(((own_ref.at[1], place.blk), (later_ref, place.far))):
            remote(source, panel_ref.at[slot], near_send.at[0], near_recv.at[0], place.sibling).start()
            mine.append(pltpu.make_async_copy(source, panel_ref.at[slot], own_sems.at[number]))
            mine[-1].start()
        for j, target in partners().items():
            copies.append(remote(slot_ref, rslot_ref.at[j - 1], slot_send.at[j - 1], slot_recv.at[j - 1], target))
            copies[-1].start()

    between = {0: rest}
    for n, blank in enumerate((blank0, blank1, blank2, blank3)):
        between[30 + 20 * n] = functools.partial(clear, blank)
    spread(place, panel_ref, ORDER_B, start, (send_sem, recv_sems, near_send, near_recv), between)
    for copy in mine:
        copy.wait()
    settle(panel_ref, 30, send_sem.at[0])
    settle(panel_ref, 32, near_send.at[0])
    settle(panel_ref, 32, near_recv.at[0])
    for copy in copies:
        copy.wait()


def swap_kernel(send_ref, recv_ref, blank0, blank1, blank2, blank3, swap_send, swap_recv):
    greet(list(partners().values()))
    copies = swap(send_ref, recv_ref, (swap_send, swap_recv))
    for blank in (blank0, blank1, blank2, blank3):
        clear(blank)
    for copy in copies:
        copy.wait()


ORDER_A = arrival_order(slot=0.73, latency=3.0, far_slot=1.5, far_latency=5.0)
ORDER_B = arrival_order(slot=0.73, far_slot=0.0, far_latency=0.0)
ANYWHERE = pl.BlockSpec(memory_space=pl.ANY)
PANEL = jax.ShapeDtypeStruct((NBLK, RF, ROWS, 128), jnp.bfloat16)
BLANK = jax.ShapeDtypeStruct((POS * LOW, 128), jnp.float32)
GATHER_VMEM = 20 << 20
RECV = jax.ShapeDtypeStruct((3, CAP, LOW, 128), jnp.bfloat16)
ONE = pltpu.SemaphoreType.DMA((1,))
TWO = pltpu.SemaphoreType.DMA((2,))
THREE = pltpu.SemaphoreType.DMA((3,))
MANY = pltpu.SemaphoreType.DMA((len(PIECES),))


def gather(own, a_tiles, p_tiles):
    vmem = pl.BlockSpec(memory_space=pltpu.VMEM)
    return pl.pallas_call(
        gather_kernel,
        out_shape=(
            PANEL,
            jax.ShapeDtypeStruct((RF, ROWS, 128), jnp.bfloat16),
            jax.ShapeDtypeStruct((SLOTS, 128, 128), jnp.bfloat16),
            jax.ShapeDtypeStruct((RF, 128, 512), jnp.bfloat16),
            *[BLANK] * NACC,
        ),
        in_specs=[ANYWHERE] + [pl.BlockSpec(memory_space=pltpu.HBM)] * 2,
        out_specs=(ANYWHERE, ANYWHERE, vmem, vmem, *[vmem] * NACC),
        scratch_shapes=[
            ONE, MANY, ONE, ONE, pltpu.SemaphoreType.DMA((4,)), pltpu.SemaphoreType.DMA((8,)), ONE, TWO,
            pltpu.VMEM((4, 2, ROWS, 128), jnp.bfloat16),
            pltpu.VMEM((2, 4, ROWS, 128), jnp.bfloat16),
            pltpu.VMEM((RF, TILE, KA * TILE), jnp.bfloat16),
            pltpu.VMEM((RF, TILE, KP * TILE), jnp.bfloat16),
        ],
        compiler_params=pltpu.CompilerParams(collective_id=0, has_side_effects=True, vmem_limit_bytes=GATHER_VMEM),
        cost_estimate=pl.CostEstimate(flops=0, transcendentals=0, bytes_accessed=1 << 26),
        name="gather",
    )(own, a_tiles, p_tiles)


def gather_swap(own, later, send, slots):
    vmem = pl.BlockSpec(memory_space=pltpu.VMEM)
    return pl.pallas_call(
        gather_swap_kernel,
        out_shape=(PANEL, RECV, jax.ShapeDtypeStruct((3, 2, 128), jnp.int32), *[BLANK] * NACC),
        in_specs=[ANYWHERE] * 4,
        out_specs=(ANYWHERE, ANYWHERE, ANYWHERE, *[vmem] * NACC),
        scratch_shapes=[ONE, MANY, ONE, ONE, TWO, THREE, THREE, THREE, THREE],
        compiler_params=pltpu.CompilerParams(collective_id=1, has_side_effects=True, vmem_limit_bytes=GATHER_VMEM),
        cost_estimate=pl.CostEstimate(flops=0, transcendentals=0, bytes_accessed=1 << 26),
        name="gather_swap",
    )(own, later, send, slots)


def exchange(send):
    return pl.pallas_call(
        swap_kernel,
        out_shape=(RECV, *[BLANK] * 4),
        in_specs=[ANYWHERE],
        out_specs=(ANYWHERE, *[pl.BlockSpec(memory_space=pltpu.VMEM)] * 4),
        scratch_shapes=[THREE, THREE],
        compiler_params=pltpu.CompilerParams(collective_id=2, has_side_effects=True, vmem_limit_bytes=12 << 20),
        name="exchange",
    )(send)


def arrange_kernel(p_hbm, route_hbm, cols_hbm, out_ref, line_ref, p_ref, route_ref, cols_ref, sems):
    copies = [
        pltpu.make_async_copy(source, target, sems.at[number])
        for number, (source, target) in enumerate(((p_hbm, p_ref), (route_hbm, route_ref), (cols_hbm, cols_ref)))
    ]
    for copy in copies:
        copy.start()
    for copy in copies:
        copy.wait()
    line_ref[2 * RF:3 * RF, :] = jnp.zeros((RF, 128), jnp.int32)
    line_ref[2 * RF:3 * RF, 0:KA] = cols_ref[...]
    for half in range(2):
        line_ref[pl.ds(half, RF, stride=2), :] = route_ref[:, half * 128:(half + 1) * 128] * LOW
    group = lax.broadcasted_iota(jnp.int32, (TILE, 128), 1) // 32

    def merged(parts):
        value = parts[0]
        for number in (1, 2, 3):
            value = jnp.where(group == number, parts[number], value)
        return value

    @pl.loop(0, RF)
    def _(i):
        left = p_ref[i, :, 0:128].astype(jnp.float32)
        right = p_ref[i, :, 128:256].astype(jnp.float32)
        first = merged([left, pltpu.roll(left, 96, 1), pltpu.roll(right, 64, 1), pltpu.roll(right, 32, 1)])
        second = merged([pltpu.roll(left, 96, 1), pltpu.roll(left, 64, 1), pltpu.roll(right, 32, 1), right])
        block = jnp.concatenate([first, second], axis=0).T.astype(jnp.bfloat16)
        for q in range(KP):
            for part in range(2):
                out_ref[part, i, q * LOW:(q + 1) * LOW, :] = block[q * 32 + part * LOW:q * 32 + (part + 1) * LOW]


def arranged(*arrays):
    vmem = pl.BlockSpec(memory_space=pltpu.VMEM)
    return pl.pallas_call(
        arrange_kernel,
        out_shape=(
            jax.ShapeDtypeStruct((2, RF, ROWS, 128), jnp.bfloat16),
            jax.ShapeDtypeStruct((3 * RF, 128), jnp.int32),
        ),
        in_specs=[pl.BlockSpec(memory_space=pltpu.HBM)] * 3,
        out_specs=(vmem, vmem),
        scratch_shapes=[
            pltpu.VMEM((RF, TILE, KP * TILE), jnp.bfloat16),
            pltpu.VMEM((RF, 256), jnp.int32),
            pltpu.VMEM((RF, KA), jnp.int32),
            THREE,
        ],
        compiler_params=pltpu.CompilerParams(vmem_limit_bytes=4 * 1024 * 1024),
        name="arrange",
    )(*[pltpu.with_memory_space_constraint(array, pltpu.HBM) for array in arrays])


def body(a_tiles, a_cols, p_tiles, route_list, out_slot):
    me = lax.axis_index("grp").astype(jnp.int32).reshape(1)
    slots = out_slot.reshape(2, 128)
    arranged_tiles, lines = arranged(p_tiles, route_list, a_cols)
    lines = lines.reshape(3 * RF * 128)
    a_tiles = pltpu.with_memory_space_constraint(a_tiles, pltpu.HBM)
    p_tiles = pltpu.with_memory_space_constraint(p_tiles, pltpu.HBM)
    panel0, later, tiles, weights, *blank0 = gather(arranged_tiles, a_tiles, p_tiles)
    send0, own0 = product(lines, me, tiles, weights, panel0.reshape(NBLK * RF, ROWS, 128), blank0)
    panel1, recv0, rslots, *blank1 = gather_swap(
        arranged_tiles, later, send0, pltpu.with_memory_space_constraint(slots, pltpu.HBM))
    send1, own1 = product(lines, me, tiles, weights, panel1.reshape(NBLK * RF, ROWS, 128), blank1)
    recv1, *blank = exchange(send1)
    out = collect(slots.reshape(POS), rslots.reshape(3 * POS), me, own0, own1, recv0, recv1, blank)
    return out.reshape(16, 32, 8, 128).transpose(0, 2, 1, 3).reshape(OSLOT, TILE * TILE)


def solution(mesh):
    in_specs = (
        P(("blk", "grp"), None, None),
        P(("blk", "grp"), None),
        P(("blk", "grp"), None, None),
        P(("blk", "grp"), None),
        P(("blk", "grp"), None),
    )
    out_specs = P(("blk", "grp"), None)
    return jax.shard_map(body, mesh=mesh, in_specs=in_specs, out_specs=out_specs, check_vma=False)
```

```python
import functools
import heapq

import jax
import jax.numpy as jnp
from jax import lax
from jax.experimental import pallas as pl
from jax.experimental.pallas import tpu as pltpu
from jax.sharding import PartitionSpec as P

TILE = 64
RF = 8
KA = 16
KP = 4
CAP = 64
OSLOT = 128
GRP = 4
SLOTS = RF * KA
POS = GRP * CAP
MESH = pl.DeviceIdType.MESH
NACC = 4
LOW = 16
ROWS = KP * LOW
WUN = 16


def low_lanes(shape):
    return lax.broadcasted_iota(jnp.int32, shape, 1) < TILE


def turned(block):
    return pltpu.roll(block.astype(jnp.float32), TILE, 1).astype(jnp.bfloat16)


def build_weights(p_ref, weights):
    low = low_lanes((TILE, 128))
    zero = jnp.zeros((TILE, 128), jnp.bfloat16)

    @pl.loop(0, RF)
    def _(i):
        for half in range(2):
            pair = p_ref[i, :, half * 128:(half + 1) * 128]
            back = turned(pair)
            even, odd = 2 * half * 128, (2 * half + 1) * 128
            weights[i, 0:TILE, even:even + 128] = jnp.where(low, pair, zero)
            weights[i, TILE:128, even:even + 128] = jnp.where(low, zero, back)
            weights[i, 0:TILE, odd:odd + 128] = jnp.where(low, back, zero)
            weights[i, TILE:128, odd:odd + 128] = jnp.where(low, zero, pair)


def build_tiles(a_ref, tiles_ref, i):
    low = low_lanes((TILE, 128))
    zero = jnp.zeros((TILE, 128), jnp.bfloat16)

    @pl.loop(0, KA // 2)
    def _(kk):
        pair = a_ref[i, :, pl.ds(pl.multiple_of(kk * 128, 128), 128)]
        back = turned(pair)
        for parity in range(2):
            first, second = (pair, back) if parity == 0 else (back, pair)
            m = i * KA + kk * 2 + parity
            tiles_ref[m, 0:TILE, :] = jnp.where(low, first, zero)
            tiles_ref[m, TILE:128, :] = jnp.where(low, zero, second)


def product_kernel(lines_ref, me_ref, tiles_ref, weights, panel_ref, blank0, blank1, blank2, blank3, send_ref,
                   own_ref, acc0, acc1, acc2, acc3, ys):
    accs = (acc0, acc1, acc2, acc3)

    @pl.loop(0, RF)
    def _(i):
        for k in range(KA):
            m = i * KA + k
            col = lines_ref[2 * RF * 128 + i * 128 + k]
            ys[m] = lax.dot_general(
                panel_ref[(col >> 5) * RF + (col & 7)], tiles_ref[m], (((1,), (1,)), ((), ())), preferred_element_type=jnp.float32
            ).astype(jnp.bfloat16)

    @pl.loop(0, SLOTS // WUN)
    def _(step):
        i = step // (KA // WUN)
        k0 = lax.rem(step, KA // WUN) * WUN
        base = i * 256 + k0 * KP
        y = ys[pl.ds(step * WUN, WUN)].reshape(WUN * ROWS, 128)
        w = [
            jnp.dot(y, weights[i, :, sp * 256:(sp + 1) * 256], preferred_element_type=jnp.float32)
            for sp in range(2)
        ]
        for u in range(WUN):
            for q in range(KP):
                for s in range(KP):
                    r = lines_ref[base + (s * KA + u) * KP + q]
                    acc = accs[s % NACC]
                    row, lane = u * ROWS + q * LOW, s % 2 * 128
                    here = pl.ds(pl.multiple_of(r, LOW), LOW)
                    acc[here, :] = acc[here, :] + w[s // 2][row:row + LOW, lane:lane + 128]

    def total(r, count):
        here = pl.ds(pl.multiple_of(r * LOW, LOW), count * LOW)
        value = (accs[0][here, :] + accs[1][here, :]) + (accs[2][here, :] + accs[3][here, :])
        return value.reshape(count, LOW, 128)

    @pl.loop(0, POS // 4)
    def _(step):
        send_ref[pl.ds(step * 4, 4)] = total(step * 4, 4).astype(jnp.bfloat16)

    @pl.loop(0, CAP // 4)
    def _(step):
        own_ref[pl.ds(step * 4, 4)] = total(me_ref[0] * CAP + step * 4, 4)


def product(lines, me, tiles, weights, panel, blanks):
    smem = pl.BlockSpec(memory_space=pltpu.SMEM)
    vmem = pl.BlockSpec(memory_space=pltpu.VMEM)
    return pl.pallas_call(
        product_kernel,
        out_shape=(
            jax.ShapeDtypeStruct((POS, LOW, 128), jnp.bfloat16),
            jax.ShapeDtypeStruct((CAP, LOW, 128), jnp.float32),
            *[BLANK] * NACC,
        ),
        in_specs=[smem, smem, vmem, vmem, vmem, *[vmem] * NACC],
        out_specs=(vmem, vmem, *[vmem] * NACC),
        scratch_shapes=[pltpu.VMEM((SLOTS, ROWS, 128), jnp.bfloat16)],
        input_output_aliases={5 + n: 2 + n for n in range(NACC)},
        compiler_params=pltpu.CompilerParams(vmem_limit_bytes=16 * 1024 * 1024),
        name="product",
    )(lines, me, tiles, weights, panel, *blanks)[:2]


def collect_kernel(slot_ref, rslot_ref, me_ref, own0_ref, own1_ref, recv0_ref, recv1_ref, blank0, blank1, blank2, blank3,
                   out_hbm, acc0, acc1, acc2, acc3, flipped, out_ref, out_sems):
    accs = (acc0, acc1, acc2, acc3)
    me = me_ref[0]

    @pl.loop(0, CAP // 2)
    def _(step):
        for e in range(2):
            p = step * 2 + e
            for j in range(4):
                b = slot_ref[me * CAP + p] if j == 3 else rslot_ref[j * POS + me * CAP + p]
                low = own0_ref[p] if j == 3 else recv0_ref[j, p].astype(jnp.float32)
                high = own1_ref[p] if j == 3 else recv1_ref[j, p].astype(jnp.float32)
                here = pl.ds(pl.multiple_of(b * 32, 32), LOW)
                there = pl.ds(pl.multiple_of(b * 32 + LOW, LOW), LOW)
                accs[j][here, :] = accs[j][here, :] + low
                accs[j][there, :] = accs[j][there, :] + high

    lane = lax.broadcasted_iota(jnp.int32, (32, 128), 1)
    low = lane < 64
    even = lax.rem(lane // 32, 2) == 0

    def leave(g):
        part = pl.ds(pl.multiple_of(g * 512, 512), 512)
        return pltpu.make_async_copy(out_ref.at[part, :], out_hbm.at[part, :], out_sems.at[g])

    @pl.loop(0, OSLOT // 16)
    def _(g):
        @pl.when(g > 0)
        def _():
            leave(g - 1).start()

        quads = range(4)
        for quad in quads:
            here = pl.ds(pl.multiple_of(g * 512 + quad * 128, 128), 128)
            block = (accs[0][here, :] + accs[1][here, :]) + (accs[2][here, :] + accs[3][here, :])
            flipped[quad] = block.T
        for quad in quads:
            parts = [
                flipped[quad, pl.ds(half * 64 + parity, 32, stride=2), :]
                for parity in range(2) for half in range(2)
            ]
            mid = [None] * 4
            for n in range(2):
                a, b = parts[n], parts[n + 2]
                mid[n] = jnp.where(low, a, pltpu.roll(b, 64, 1))
                mid[n + 2] = jnp.where(low, pltpu.roll(a, 64, 1), b)
            for n in range(2):
                a, b = mid[2 * n], mid[2 * n + 1]
                first = jnp.where(even, a, pltpu.roll(b, 32, 1))
                second = jnp.where(even, pltpu.roll(a, 96, 1), b)
                for which, value in ((2 * n, first), (2 * n + 1, second)):
                    row = g * 512 + quad // 2 * 256 + quad % 2 * 4 + which
                    out_ref[pl.ds(row, 32, stride=8), :] = value

    for g in range(OSLOT // 16 - 1):
        leave(g).wait()
    last = leave(OSLOT // 16 - 1)
    last.start()
    last.wait()


def collect(slots, rslots, me, own0, own1, recv0, recv1, blanks):
    smem = pl.BlockSpec(memory_space=pltpu.SMEM)
    vmem = pl.BlockSpec(memory_space=pltpu.VMEM)
    return pl.pallas_call(
        collect_kernel,
        out_shape=(jax.ShapeDtypeStruct((OSLOT * 32, 128), jnp.float32), *[BLANK] * 4),
        in_specs=[smem, smem, smem, vmem, vmem, vmem, vmem, *[vmem] * 4],
        out_specs=(pl.BlockSpec(memory_space=pltpu.HBM), *[vmem] * 4),
        scratch_shapes=[
            pltpu.VMEM((4, 128, 128), jnp.float32),
            pltpu.VMEM((OSLOT * 32, 128), jnp.float32),
            pltpu.SemaphoreType.DMA((OSLOT // 16,)),
        ],
        input_output_aliases={7 + n: 1 + n for n in range(4)},
        compiler_params=pltpu.CompilerParams(vmem_limit_bytes=16 * 1024 * 1024),
        name="collect",
    )(slots, rslots, me, own0, own1, recv0, recv1, *blanks)[0]


NBLK = 64
STEPS = (0, 1, -1, 2)
PIECES = [
    (layer, first, turn, along, across)
    for layer in (0, 1) for first in (0, 1) for turn in (0, 1) for along in STEPS for across in STEPS
]
PIECE_ID = {piece: number for number, piece in enumerate(PIECES)}


def next_hops(piece):
    layer, first, turn, along, across = piece
    dims = ("x", "y") if first == 0 else ("y", "x")
    sign = 1 - 2 * turn
    hops = []
    if across == 0:
        if along == 0:
            hops += [(dims[0], sign, (layer, first, turn, 1, 0)), (dims[0], -sign, (layer, first, turn, -1, 0))]
        if along == 1:
            hops += [(dims[0], sign, (layer, first, turn, 2, 0))]
        hops += [(dims[1], sign, (layer, first, turn, along, 1)), (dims[1], -sign, (layer, first, turn, along, -1))]
    elif across == 1:
        hops += [(dims[1], sign, (layer, first, turn, along, 2))]
    return hops


def arrival_order(slot=1.46, latency=2.0, far_slot=5.8, far_latency=4.0, issue=0.05):
    heap, order, free, clock, count = [], [], {}, 0.0, 0
    for layer in (0, 1):
        for number, (first, turn) in enumerate(((0, 0), (0, 1), (1, 0), (1, 1))):
            when = 0.0 if layer == 0 else (number + 1) * far_slot + far_latency
            heapq.heappush(heap, (when, 0, count, (layer, first, turn, 0, 0)))
            count += 1
    while heap:
        when, _, _, piece = heapq.heappop(heap)
        clock = max(clock, when)
        order.append(piece)
        for dim, sign, after in next_hops(piece):
            clock += issue
            free[dim, sign] = max(clock, free.get((dim, sign), 0.0)) + slot
            heapq.heappush(heap, (free[dim, sign] + latency, -len(next_hops(after)), count, after))
            count += 1
        clock += issue
    return order


def remote(src, dst, send_sem, recv_sem, target):
    return pltpu.make_async_remote_copy(
        src_ref=src, dst_ref=dst, send_sem=send_sem, recv_sem=recv_sem, device_id=target, device_id_type=MESH)


def partners():
    blk, me = lax.axis_index("blk"), lax.axis_index("grp")
    return {1: (blk, me + 1 - 2 * lax.rem(me, 2)), 2: (blk, lax.rem(me + 2, 4)), 3: (blk, 3 - me)}


class Place:
    def __init__(self):
        self.blk, self.grp = lax.axis_index("blk"), lax.axis_index("grp")
        self.core = lax.rem(self.blk, 2)
        self.at = {"x": lax.rem(self.blk // 2, 4), "y": lax.rem(self.blk // 8, 4)}
        self.high = self.blk // 32
        self.sibling = (self.number(self.high, self.at, 1 - self.core), self.grp)
        self.far = self.number(1 - self.high, self.at, self.core)
        self.opposite = (self.far, self.grp)
        self.neighbours = {
            (dim, sign): (self.moved(dim, sign), self.grp) for dim in ("x", "y") for sign in (1, -1)
        }

    def number(self, high, at, core):
        return ((high * 4 + at["y"]) * 4 + at["x"]) * 2 + core

    def moved(self, dim, by):
        at = dict(self.at)
        at[dim] = lax.rem(at[dim] + by + 4, 4)
        return self.number(self.high, at, self.core)

    def origin(self, piece):
        layer, first, turn, along, across = piece
        sign = 1 - 2 * turn
        dims = ("x", "y") if first == 0 else ("y", "x")
        at = dict(self.at)
        at[dims[0]] = lax.rem(at[dims[0]] - sign * along + 4, 4)
        at[dims[1]] = lax.rem(at[dims[1]] - sign * across + 4, 4)
        return self.number(self.high if layer == 0 else 1 - self.high, at, self.core)


def greet(targets):
    barrier = pltpu.get_barrier_semaphore()
    for target in targets:
        pl.semaphore_signal(barrier, inc=1, device_id=target, device_id_type=MESH)
    pl.semaphore_wait(barrier, len(targets))


def rows(piece):
    return pl.ds(2 * (2 * piece[1] + piece[2]), 2)


def settle(ref, count, sem):
    part = ref.at[pl.ds(0, count)]
    pltpu.make_async_copy(part, part, sem).wait()


def spread(place, panel_ref, order, start, sems, between):
    send_sem, recv_sems, near_send, near_recv = sems

    def held(piece):
        return panel_ref.at[place.origin(piece), rows(piece)]

    for piece in start:
        source = start[piece]
        for dim, sign, after in next_hops(piece):
            remote(source, held(piece), send_sem.at[0], recv_sems.at[PIECE_ID[after]], place.neighbours[dim, sign]).start()
    count = 0
    for piece in order:
        if piece in start:
            continue
        if count in between:
            between[count]()
        count += 1
        here = held(piece)
        remote(here, here, send_sem.at[0], recv_sems.at[PIECE_ID[piece]], place.sibling).wait_recv()
        for dim, sign, after in next_hops(piece):
            remote(here, here, send_sem.at[0], recv_sems.at[PIECE_ID[after]], place.neighbours[dim, sign]).start()
        remote(here, here, near_send.at[0], near_recv.at[0], place.sibling).start()


ORIGINS = [(first, turn, 0, 0) for first, turn in ((0, 0), (0, 1), (1, 0), (1, 1))]


def clear(ref):
    @pl.loop(0, POS * LOW // 64)
    def _(step):
        ref[pl.ds(pl.multiple_of(step * 64, 64), 64), :] = jnp.zeros((64, 128), jnp.float32)


def gather_kernel(own_ref, a_hbm, p_hbm, panel_ref, later_ref, tiles_ref, weights_ref, blank0, blank1, blank2, blank3, send_sem, recv_sems, near_send,
                  near_recv, first_sems, later_sems, own_sem, a_sem, transit, later_transit, a_ref, p_ref):
    place = Place()
    z = place.high * 4 + place.grp

    def above(by):
        level = lax.rem(z + by + 8, 8)
        return place.number(level // 4, place.at, place.core), lax.rem(level, 4)

    fetch = pltpu.make_async_copy(a_hbm, a_ref, a_sem.at[0])
    fetch.start()
    fetch_p = pltpu.make_async_copy(p_hbm, p_ref, a_sem.at[1])
    fetch_p.start()
    greet([place.sibling, above(1), above(-1), above(3), above(-3), *place.neighbours.values()])
    start = {(0,) + piece: own_ref.at[0, rows((0,) + piece)] for piece in ORIGINS}
    sems = (send_sem, recv_sems, near_send, near_recv)
    for number, piece in enumerate(start):
        remote(start[piece], transit.at[number], send_sem.at[0], first_sems.at[number], above(1 - 2 * piece[2])).start()
    lates = []

    def first_leg():
        remote(own_ref.at[0], panel_ref.at[place.blk], near_send.at[0], near_recv.at[0], place.sibling).start()
        pltpu.make_async_copy(own_ref.at[0], panel_ref.at[place.blk], own_sem.at[0]).start()
        for number, piece in enumerate(start):
            up = 1 - 2 * piece[2]
            remote(transit.at[number], transit.at[number], send_sem.at[0], first_sems.at[number], above(up)).wait_recv()
            remote(transit.at[number], panel_ref.at[above(-up)[0], rows(piece)], send_sem.at[0],
                   recv_sems.at[PIECE_ID[(1,) + piece[1:]]], above(3 * up)).start()
        for turn in range(2):
            part = pl.ds(4 * turn, 4)
            lates.append(remote(own_ref.at[1, part], later_transit.at[turn], later_sems.at[turn], later_sems.at[2 + turn],
                                above(1 - 2 * turn)))
            lates[-1].start()

    def second_leg():
        for turn in range(2):
            lates[turn].wait_recv()
            lates.append(remote(later_transit.at[turn], later_ref.at[pl.ds(4 * turn, 4)], later_sems.at[4 + turn],
                                later_sems.at[6 + turn], above(3 * (1 - 2 * turn))))
            lates[-1].start()

    between = {0: first_leg, 30: second_leg, 40: fetch.wait}

    def weights():
        fetch_p.wait()
        build_weights(p_ref, weights_ref)

    between[36] = weights
    for i in range(RF):
        between[44 + 8 * i] = functools.partial(build_tiles, a_ref, tiles_ref, i)
    for n, blank in enumerate((blank0, blank1, blank2, blank3)):
        between[50 + 16 * n] = functools.partial(clear, blank)
    spread(place, panel_ref, ORDER_A, start, sems, between)
    pltpu.make_async_copy(own_ref.at[0], panel_ref.at[place.blk], own_sem.at[0]).wait()
    for turn in range(2):
        lates[turn].wait_send()
        lates[2 + turn].wait()
    settle(panel_ref, 32, send_sem.at[0])
    settle(panel_ref, 32, near_send.at[0])
    settle(panel_ref, 32, near_recv.at[0])


def swap(send_ref, recv_ref, sems):
    send_sems, recv_sems = sems
    copies = []
    for j, target in reversed(partners().items()):
        copies.append(remote(
            send_ref.at[pl.ds(target[1] * CAP, CAP)], recv_ref.at[j - 1], send_sems.at[j - 1], recv_sems.at[j - 1],
            target))
        copies[-1].start()
    return copies


def gather_swap_kernel(own_ref, later_ref, send_ref, slot_ref, panel_ref, recv_ref, rslot_ref, blank0, blank1, blank2,
                       blank3, send_sem, recv_sems,
                       near_send, near_recv, own_sems, swap_send, swap_recv, slot_send, slot_recv):
    place = Place()
    greet([place.sibling, *place.neighbours.values(), *partners().values()])
    copies = swap(send_ref, recv_ref, (swap_send, swap_recv))
    start = {(0,) + piece: own_ref.at[1, rows((0,) + piece)] for piece in ORIGINS}
    start |= {(1,) + piece: later_ref.at[rows((1,) + piece)] for piece in ORIGINS}
    mine = []

    def rest():
        for number, (source, slot) in enumerate(((own_ref.at[1], place.blk), (later_ref, place.far))):
            remote(source, panel_ref.at[slot], near_send.at[0], near_recv.at[0], place.sibling).start()
            mine.append(pltpu.make_async_copy(source, panel_ref.at[slot], own_sems.at[number]))
            mine[-1].start()
        for j, target in partners().items():
            copies.append(remote(slot_ref, rslot_ref.at[j - 1], slot_send.at[j - 1], slot_recv.at[j - 1], target))
            copies[-1].start()

    between = {0: rest}
    for n, blank in enumerate((blank0, blank1, blank2, blank3)):
        between[30 + 20 * n] = functools.partial(clear, blank)
    spread(place, panel_ref, ORDER_B, start, (send_sem, recv_sems, near_send, near_recv), between)
    for copy in mine:
        copy.wait()
    settle(panel_ref, 30, send_sem.at[0])
    settle(panel_ref, 32, near_send.at[0])
    settle(panel_ref, 32, near_recv.at[0])
    for copy in copies:
        copy.wait()


def swap_kernel(send_ref, recv_ref, blank0, blank1, blank2, blank3, swap_send, swap_recv):
    greet(list(partners().values()))
    copies = swap(send_ref, recv_ref, (swap_send, swap_recv))
    for blank in (blank0, blank1, blank2, blank3):
        clear(blank)
    for copy in copies:
        copy.wait()


ORDER_A = arrival_order(slot=0.73, latency=3.0, far_slot=1.5, far_latency=5.0)
ORDER_B = arrival_order(slot=0.73, far_slot=0.0, far_latency=0.0)
ANYWHERE = pl.BlockSpec(memory_space=pl.ANY)
PANEL = jax.ShapeDtypeStruct((NBLK, RF, ROWS, 128), jnp.bfloat16)
BLANK = jax.ShapeDtypeStruct((POS * LOW, 128), jnp.float32)
GATHER_VMEM = 20 << 20
RECV = jax.ShapeDtypeStruct((3, CAP, LOW, 128), jnp.bfloat16)
ONE = pltpu.SemaphoreType.DMA((1,))
TWO = pltpu.SemaphoreType.DMA((2,))
THREE = pltpu.SemaphoreType.DMA((3,))
MANY = pltpu.SemaphoreType.DMA((len(PIECES),))


def gather(own, a_tiles, p_tiles):
    vmem = pl.BlockSpec(memory_space=pltpu.VMEM)
    return pl.pallas_call(
        gather_kernel,
        out_shape=(
            PANEL,
            jax.ShapeDtypeStruct((RF, ROWS, 128), jnp.bfloat16),
            jax.ShapeDtypeStruct((SLOTS, 128, 128), jnp.bfloat16),
            jax.ShapeDtypeStruct((RF, 128, 512), jnp.bfloat16),
            *[BLANK] * NACC,
        ),
        in_specs=[ANYWHERE] + [pl.BlockSpec(memory_space=pltpu.HBM)] * 2,
        out_specs=(ANYWHERE, ANYWHERE, vmem, vmem, *[vmem] * NACC),
        scratch_shapes=[
            ONE, MANY, ONE, ONE, pltpu.SemaphoreType.DMA((4,)), pltpu.SemaphoreType.DMA((8,)), ONE, TWO,
            pltpu.VMEM((4, 2, ROWS, 128), jnp.bfloat16),
            pltpu.VMEM((2, 4, ROWS, 128), jnp.bfloat16),
            pltpu.VMEM((RF, TILE, KA * TILE), jnp.bfloat16),
            pltpu.VMEM((RF, TILE, KP * TILE), jnp.bfloat16),
        ],
        compiler_params=pltpu.CompilerParams(collective_id=0, has_side_effects=True, vmem_limit_bytes=GATHER_VMEM),
        cost_estimate=pl.CostEstimate(flops=0, transcendentals=0, bytes_accessed=1 << 26),
        name="gather",
    )(own, a_tiles, p_tiles)


def gather_swap(own, later, send, slots):
    vmem = pl.BlockSpec(memory_space=pltpu.VMEM)
    return pl.pallas_call(
        gather_swap_kernel,
        out_shape=(PANEL, RECV, jax.ShapeDtypeStruct((3, 2, 128), jnp.int32), *[BLANK] * NACC),
        in_specs=[ANYWHERE] * 4,
        out_specs=(ANYWHERE, ANYWHERE, ANYWHERE, *[vmem] * NACC),
        scratch_shapes=[ONE, MANY, ONE, ONE, TWO, THREE, THREE, THREE, THREE],
        compiler_params=pltpu.CompilerParams(collective_id=1, has_side_effects=True, vmem_limit_bytes=GATHER_VMEM),
        cost_estimate=pl.CostEstimate(flops=0, transcendentals=0, bytes_accessed=1 << 26),
        name="gather_swap",
    )(own, later, send, slots)


def exchange(send):
    return pl.pallas_call(
        swap_kernel,
        out_shape=(RECV, *[BLANK] * 4),
        in_specs=[ANYWHERE],
        out_specs=(ANYWHERE, *[pl.BlockSpec(memory_space=pltpu.VMEM)] * 4),
        scratch_shapes=[THREE, THREE],
        compiler_params=pltpu.CompilerParams(collective_id=2, has_side_effects=True, vmem_limit_bytes=12 << 20),
        name="exchange",
    )(send)


def arrange_kernel(p_hbm, route_hbm, cols_hbm, out_ref, line_ref, p_ref, route_ref, cols_ref, sems):
    copies = [
        pltpu.make_async_copy(source, target, sems.at[number])
        for number, (source, target) in enumerate(((p_hbm, p_ref), (route_hbm, route_ref), (cols_hbm, cols_ref)))
    ]
    for copy in copies:
        copy.start()
    for copy in copies:
        copy.wait()
    line_ref[2 * RF:3 * RF, :] = jnp.zeros((RF, 128), jnp.int32)
    line_ref[2 * RF:3 * RF, 0:KA] = cols_ref[...]
    for half in range(2):
        line_ref[pl.ds(half, RF, stride=2), :] = route_ref[:, half * 128:(half + 1) * 128] * LOW
    group = lax.broadcasted_iota(jnp.int32, (TILE, 128), 1) // 32

    def merged(parts):
        value = parts[0]
        for number in (1, 2, 3):
            value = jnp.where(group == number, parts[number], value)
        return value

    @pl.loop(0, RF // 2)
    def _(step):
        for e in range(2):
            i = step * 2 + e
            left = p_ref[i, :, 0:128].astype(jnp.float32)
            right = p_ref[i, :, 128:256].astype(jnp.float32)
            first = merged([left, pltpu.roll(left, 96, 1), pltpu.roll(right, 64, 1), pltpu.roll(right, 32, 1)])
            second = merged([pltpu.roll(left, 96, 1), pltpu.roll(left, 64, 1), pltpu.roll(right, 32, 1), right])
            block = jnp.concatenate([first, second], axis=0).T.astype(jnp.bfloat16)
            for q in range(KP):
                for part in range(2):
                    out_ref[part, i, q * LOW:(q + 1) * LOW, :] = block[q * 32 + part * LOW:q * 32 + (part + 1) * LOW]


def arranged(*arrays):
    vmem = pl.BlockSpec(memory_space=pltpu.VMEM)
    return pl.pallas_call(
        arrange_kernel,
        out_shape=(
            jax.ShapeDtypeStruct((2, RF, ROWS, 128), jnp.bfloat16),
            jax.ShapeDtypeStruct((3 * RF, 128), jnp.int32),
        ),
        in_specs=[pl.BlockSpec(memory_space=pltpu.HBM)] * 3,
        out_specs=(vmem, vmem),
        scratch_shapes=[
            pltpu.VMEM((RF, TILE, KP * TILE), jnp.bfloat16),
            pltpu.VMEM((RF, 256), jnp.int32),
            pltpu.VMEM((RF, KA), jnp.int32),
            THREE,
        ],
        compiler_params=pltpu.CompilerParams(vmem_limit_bytes=4 * 1024 * 1024),
        name="arrange",
    )(*[pltpu.with_memory_space_constraint(array, pltpu.HBM) for array in arrays])


def body(a_tiles, a_cols, p_tiles, route_list, out_slot):
    me = lax.axis_index("grp").astype(jnp.int32).reshape(1)
    slots = out_slot.reshape(2, 128)
    arranged_tiles, lines = arranged(p_tiles, route_list, a_cols)
    lines = lines.reshape(3 * RF * 128)
    a_tiles = pltpu.with_memory_space_constraint(a_tiles, pltpu.HBM)
    p_tiles = pltpu.with_memory_space_constraint(p_tiles, pltpu.HBM)
    panel0, later, tiles, weights, *blank0 = gather(arranged_tiles, a_tiles, p_tiles)
    send0, own0 = product(lines, me, tiles, weights, panel0.reshape(NBLK * RF, ROWS, 128), blank0)
    panel1, recv0, rslots, *blank1 = gather_swap(
        arranged_tiles, later, send0, pltpu.with_memory_space_constraint(slots, pltpu.HBM))
    send1, own1 = product(lines, me, tiles, weights, panel1.reshape(NBLK * RF, ROWS, 128), blank1)
    recv1, *blank = exchange(send1)
    out = collect(slots.reshape(POS), rslots.reshape(3 * POS), me, own0, own1, recv0, recv1, blank)
    return out.reshape(16, 32, 8, 128).transpose(0, 2, 1, 3).reshape(OSLOT, TILE * TILE)


def solution(mesh):
    in_specs = (
        P(("blk", "grp"), None, None),
        P(("blk", "grp"), None),
        P(("blk", "grp"), None, None),
        P(("blk", "grp"), None),
        P(("blk", "grp"), None),
    )
    out_specs = P(("blk", "grp"), None)
    return jax.shard_map(body, mesh=mesh, in_specs=in_specs, out_specs=out_specs, check_vma=False)
```
